256 devices in a mesh: mpo: 8 (over y, core), blk: 32 (over x, z).
Axes of the slice: x: 4, y: 4, z: 8, core: 2. Of those that a mesh axis runs over, the one named last changes fastest.
Arguments:
- two_site: bfloat16 [256, 16, 128, 128], P('blk'), may hold values from -6 to 6
- left_env: bfloat16 [34, 256, 128, 128], P(None, 'blk'), may hold values from -0.5 to 0.5
- right_env: bfloat16 [34, 256, 128, 128], P(None, 'blk'), may hold values from -0.5 to 0.5
- mpo_terms: bfloat16 [64, 16, 16], P('mpo'), may hold values from -0.1875 to 0.1875
- term_left: int32 [64], P('mpo'), may hold values from 0 to 33
- term_right: int32 [64], P('mpo'), may hold values from 0 to 33
- shifts: int32 [16], replicated, may hold values from -1 to 1, as said below
- block_sizes: int32 [256], replicated, may hold values from 64 to 128, as said below
Outputs:
- applied: bfloat16 [256, 16, 128, 128], P('blk', 'mpo')
The draws below stay inside these ranges and needn't reach their ends.
Inputs may be any that keep to these rules, and one draw needn't show every extreme that they name: `shifts`: both -1 and 1 occur among the offsets. `block_sizes`: both 128 // 2 and 128 occur among the live dimensions.
All inputs are finite; a program needn't handle non-finite values.
Results may differ from the reference program's by a relative error of at most 0.0057.
Values may be sent and summed in bfloat16 or wider, within the bound.
A program may use at most 128 MiB of HBM per device.

```python
import jax
import jax.numpy as jnp
from jax import lax

W = 34
P_SIZE = 16
DB = 128
SH = 1
NL = 256
NT = 64


def draw_shifts(key, part):
    values = jax.random.randint(jax.random.fold_in(key, 11), (P_SIZE,), -SH, SH + 1)
    order = jax.random.permutation(jax.random.fold_in(key, 12), P_SIZE)
    values = values.at[order[0]].set(-SH)
    values = values.at[order[1]].set(SH)
    return values.astype(jnp.int32)


def draw_block_sizes(key, part):
    values = jax.random.randint(jax.random.fold_in(key, 21), (NL,), DB // 2, DB + 1)
    order = jax.random.permutation(jax.random.fold_in(key, 22), NL)
    values = values.at[order[0]].set(DB // 2)
    values = values.at[order[1]].set(DB)
    return values.astype(jnp.int32)


def set_ends(values, own_key, least, largest):
    longest = values.shape.index(max(values.shape))
    spots = []
    for shift in (0, 1):
        where = [jax.random.randint(jax.random.fold_in(own_key, axis), (), 0, length) for axis, length in enumerate(values.shape)]
        where[longest] = (where[longest] + shift) % values.shape[longest]
        spots.append(tuple(where))
    return values.at[spots[0]].set(least).at[spots[1]].set(largest)


def block_scale(key, shape, split, least, top_value):
    factor_of, own = 1.0, jax.random.fold_in(key, 6)
    for position, shards_of in split:
        draws = jnp.exp(jax.random.uniform(jax.random.fold_in(own, position), (shards_of,), jnp.float32, least / len(split), top_value / len(split)))
        factor_of = factor_of * jnp.repeat(draws, shape[position] // shards_of).reshape([-1 if axis == position else 1 for axis in range(len(shape))])
    return factor_of


def normal_values(stream_key, extent, scale, most, pieces=(), kind=jnp.bfloat16):
    loudness = block_scale(stream_key, extent, pieces, -0.22, 0.18) if pieces else 1.0
    drawn = jax.random.normal(stream_key, extent, jnp.float32) * scale * loudness
    return jnp.minimum(jnp.maximum(drawn, -most), most).astype(kind)


def setup_inputs(seed: int = 0) -> dict:
    arg_keys = jax.random.split(jax.random.key(seed), 9)
    return {
        "two_site": normal_values(arg_keys[0], (NL, P_SIZE, DB, DB), 1.0, 6.0, ((0, 32),)),
        "left_env": normal_values(arg_keys[1], (W, NL, DB, DB), DB ** -0.5, 0.5, ((1, 32),)),
        "right_env": normal_values(arg_keys[2], (W, NL, DB, DB), DB ** -0.5, 0.5, ((1, 32),)),
        "mpo_terms": normal_values(arg_keys[3], (NT, P_SIZE, P_SIZE), (NT * P_SIZE) ** -0.5, 0.1875, ((0, 8),)),
        "term_left": set_ends(jax.random.randint(arg_keys[4], (NT,), 0, W), jax.random.fold_in(arg_keys[4], 1), 0, W - 1).astype(jnp.int32),
        "term_right": set_ends(jax.random.randint(arg_keys[5], (NT,), 0, W), jax.random.fold_in(arg_keys[5], 1), 0, W - 1).astype(jnp.int32),
        "shifts": draw_shifts(jax.random.fold_in(arg_keys[8], 71), 0),
        "block_sizes": draw_block_sizes(jax.random.fold_in(arg_keys[8], 71), 0),
    }


def sector_mask(block_sizes, shifts, first, blocks, total, depth):
    rows_left = first + jnp.arange(blocks, dtype=jnp.int32)
    right_index = rows_left[:, None] + shifts[None, :]
    inside = (right_index >= 0) & (right_index < total)
    table = jnp.arange(total, dtype=jnp.int32)
    size_left = jnp.sum(jnp.where(rows_left[:, None] == table[None, :], block_sizes[None, :], 0), axis=1)
    size_right = jnp.sum(jnp.where(right_index[:, :, None] == table[None, None, :], block_sizes[None, None, :], 0), axis=2)
    lines = jnp.arange(depth, dtype=jnp.int32)
    keep_rows = lines[None, None, :, None] < size_left[:, None, None, None]
    keep_cols = lines[None, None, None, :] < size_right[:, :, None, None]
    return keep_rows & keep_cols & inside[:, :, None, None]


def reference(two_site, left_env, right_env, mpo_terms, term_left, term_right, shifts, block_sizes):
    mask = sector_mask(block_sizes, shifts, 0, NL, NL, DB)
    clean = jnp.where(mask, two_site, jnp.zeros_like(two_site))
    padded = jnp.pad(right_env, ((0, 0), (SH, SH), (0, 0), (0, 0)))
    starts = (shifts + SH).astype(jnp.int32)

    def one_term(summed, item):
        left_index, right_index, matrix = item
        left_block = lax.dynamic_index_in_dim(left_env, left_index, 0, keepdims=False)
        applied_left = jnp.einsum('bxy,bqyz->bqxz', left_block.astype(jnp.float32), clean.astype(jnp.float32), precision=lax.Precision.HIGHEST)
        applied_half = applied_left.astype(jnp.bfloat16)
        mixed = jnp.einsum('pq,bqxz->bpxz', matrix.astype(jnp.float32), applied_half.astype(jnp.float32), precision=lax.Precision.HIGHEST)
        mixed_half = mixed.astype(jnp.bfloat16)
        right_rows = lax.dynamic_index_in_dim(padded, right_index, 0, keepdims=False)
        gathered = jax.vmap(lambda begin: lax.dynamic_slice_in_dim(right_rows, begin, NL, 0))(starts)
        product = jnp.einsum('bpxz,pbzy->bpxy', mixed_half.astype(jnp.float32), gathered.astype(jnp.float32), precision=lax.Precision.HIGHEST)
        return summed + product, None

    summed, unused = lax.scan(one_term, jnp.zeros(two_site.shape, jnp.float32), (term_left, term_right, mpo_terms))
    return jnp.where(mask, summed, jnp.float32(0.0)).astype(jnp.bfloat16)
```

```python
import functools

import jax
import jax.numpy as jnp
from jax import lax
from jax.experimental import pallas as pl
from jax.experimental.pallas import tpu as pltpu
from jax.sharding import PartitionSpec as P

SH = 1
YT = 16


def sector_limits(block_sizes, shifts, first, blocks, total):
    rows_left = first + jnp.arange(blocks, dtype=jnp.int32)
    right_index = rows_left[:, None] + shifts[None, :]
    inside = (right_index >= 0) & (right_index < total)
    size_left = block_sizes[rows_left]
    size_right = jnp.where(inside, block_sizes[jnp.clip(right_index, 0, total - 1)], 0)
    return size_left.astype(jnp.int32), size_right.astype(jnp.int32)


def kernel(npl, nt, tl_ref, tr_ref, rowlim_ref, collim_ref, outlim_ref, sloc_ref,
           ts_ref, left_ref, kron_ref, rloc0_ref, rloc1_ref, lo_ref, hi_ref,
           out_ref, c_scr, x_scr, y_scr):
    i = pl.program_id(0)
    nb = pl.num_programs(0)
    depth = ts_ref.shape[-1]
    nq = ts_ref.shape[1]
    rows = lax.broadcasted_iota(jnp.int32, (depth, depth), 0)
    cols = lax.broadcasted_iota(jnp.int32, (depth, depth), 1)
    row_ok = rows < rowlim_ref[i]
    for q in range(nq):
        keep = row_ok & (cols < collim_ref[i * nq + q])
        c_scr[q] = jnp.where(keep, ts_ref[0, q], jnp.zeros_like(ts_ref[0, q]))

    nr = npl * nt
    rchunk = 32
    for yb in range(depth // YT):
        cy = c_scr[:, yb * YT:(yb + 1) * YT, :].reshape(nq * YT, depth)
        for rc in range(nr // rchunk):
            k = kron_ref[rc * rchunk * YT:(rc + 1) * rchunk * YT, :]
            xy = jnp.dot(k, cy, preferred_element_type=jnp.float32)
            x_scr[rc * rchunk:(rc + 1) * rchunk, yb * YT:(yb + 1) * YT, :] = (
                xy.reshape(rchunk, YT, depth).astype(x_scr.dtype))

    def left_step(t, carry):
        lt = left_ref[tl_ref[t], 0]
        xs = jnp.concatenate([x_scr[t * npl + p] for p in range(npl)], axis=1)
        yt = jnp.dot(lt, xs, preferred_element_type=jnp.float32).astype(y_scr.dtype)
        for p in range(npl):
            y_scr[p, t] = yt[:, p * depth:(p + 1) * depth]
        return carry

    lax.fori_loop(0, nt, left_step, 0)

    def right_sum(p, src):
        def step(t, acc):
            return acc + jnp.dot(y_scr[p, t], src[tr_ref[t], 0],
                                 preferred_element_type=jnp.float32)
        acc = lax.fori_loop(0, nt, step, jnp.zeros((depth, depth), jnp.float32))
        keep = row_ok & (cols < outlim_ref[i * npl + p])
        out_ref[0, p] = jnp.where(keep, acc, 0.0).astype(out_ref.dtype)

    for p, rloc in enumerate((rloc0_ref, rloc1_ref)):
        j = i + sloc_ref[p]

        @pl.when(j < 0)
        def _():
            right_sum(p, lo_ref)

        @pl.when((j >= 0) & (j < nb))
        def _():
            right_sum(p, rloc)

        @pl.when(j >= nb)
        def _():
            right_sum(p, hi_ref)


def halos(cells, axis, dim, width):
    count = lax.axis_size(axis)
    ends = count - 1
    head = lax.slice_in_dim(cells, 0, width, axis=dim)
    tail = lax.slice_in_dim(cells, cells.shape[dim] - width, cells.shape[dim], axis=dim)
    lo = lax.ppermute(tail, axis, [(i, i + 1) for i in range(ends)])
    hi = lax.ppermute(head, axis, [(i + 1, i) for i in range(ends)])
    return lo, hi


def body(two_site, left_env, right_env, mpo_terms, term_left, term_right, shifts, block_sizes):
    blocks, nq, depth, _ = two_site.shape
    width = left_env.shape[0]
    nmpo = lax.axis_size("mpo")
    npl = nq // nmpo
    total = blocks * lax.axis_size("blk")
    first = lax.axis_index("blk") * blocks
    p_first = lax.axis_index("mpo") * npl

    terms = lax.all_gather(mpo_terms, "mpo", axis=0, tiled=True)
    tl = lax.all_gather(term_left, "mpo", axis=0, tiled=True)
    tr = lax.all_gather(term_right, "mpo", axis=0, tiled=True)
    nt = terms.shape[0]

    rowlim, collim = sector_limits(block_sizes, shifts, first, blocks, total)
    outlim = lax.dynamic_slice_in_dim(collim, p_first, npl, axis=1)
    sloc = lax.dynamic_slice_in_dim(shifts, p_first, npl)

    mine = lax.dynamic_slice_in_dim(terms, p_first, npl, axis=1).reshape(nt * npl, nq)
    eye = jnp.eye(YT, dtype=mine.dtype)
    kron = (mine[:, None, :, None] * eye[None, :, None, :]).reshape(nt * npl * YT, nq * YT)

    lo, hi = halos(right_env, "blk", 1, SH)

    rblock = (width, 1, depth, depth)

    def rloc_map(p):
        def index(b, tl_r, tr_r, rl, cl, ol, sl):
            return (0, jnp.clip(b + sl[p], 0, blocks - 1), 0, 0)
        return index

    const4 = lambda b, *refs: (0, 0, 0, 0)
    grid_spec = pltpu.PrefetchScalarGridSpec(
        num_scalar_prefetch=6,
        grid=(blocks,),
        in_specs=[
            pl.BlockSpec((1, nq, depth, depth), lambda b, *refs: (b, 0, 0, 0)),
            pl.BlockSpec(rblock, lambda b, *refs: (0, b, 0, 0)),
            pl.BlockSpec(kron.shape, lambda b, *refs: (0, 0)),
            pl.BlockSpec(rblock, rloc_map(0)),
            pl.BlockSpec(rblock, rloc_map(1)),
            pl.BlockSpec(rblock, const4),
            pl.BlockSpec(rblock, const4),
        ],
        out_specs=pl.BlockSpec((1, npl, depth, depth), lambda b, *refs: (b, 0, 0, 0)),
        scratch_shapes=[
            pltpu.VMEM((nq, depth, depth), jnp.bfloat16),
            pltpu.VMEM((nt * npl, depth, depth), jnp.bfloat16),
            pltpu.VMEM((npl, nt, depth, depth), jnp.bfloat16),
        ],
    )
    flops = 2 * blocks * (nt * npl * YT * nq * YT * depth + 2 * nt * npl * depth ** 3)
    return pl.pallas_call(
        functools.partial(kernel, npl, nt),
        out_shape=jax.ShapeDtypeStruct((blocks, npl, depth, depth), jnp.bfloat16),
        grid_spec=grid_spec,
        compiler_params=pltpu.CompilerParams(
            dimension_semantics=("arbitrary",), vmem_limit_bytes=60 * 1024 * 1024),
        cost_estimate=pl.CostEstimate(
            flops=flops, transcendentals=0,
            bytes_accessed=2 * (two_site.size + left_env.size + 3 * right_env.size)),
    )(tl, tr, rowlim, collim.reshape(-1), outlim.reshape(-1), sloc,
      two_site, left_env, kron, right_env, right_env, lo, hi)


def solution(mesh):
    return jax.shard_map(
        body,
        mesh=mesh,
        in_specs=(
            P("blk", None, None, None),
            P(None, "blk", None, None),
            P(None, "blk", None, None),
            P("mpo", None, None),
            P("mpo"),
            P("mpo"),
            P(),
            P(),
        ),
        out_specs=P("blk", "mpo", None, None),
        check_vma=False,
    )
```

```python
import functools

import jax
import jax.numpy as jnp
from jax import lax
from jax.experimental import pallas as pl
from jax.experimental.pallas import tpu as pltpu
from jax.sharding import PartitionSpec as P

SH = 1
YT = 16
UNROLL = 8
VARIANT = ""


def sector_limits(block_sizes, shifts, first, blocks, total):
    rows_left = first + jnp.arange(blocks, dtype=jnp.int32)
    right_index = rows_left[:, None] + shifts[None, :]
    inside = (right_index >= 0) & (right_index < total)
    size_left = block_sizes[rows_left]
    size_right = jnp.where(inside, block_sizes[jnp.clip(right_index, 0, total - 1)], 0)
    return size_left.astype(jnp.int32), size_right.astype(jnp.int32)


def kernel(npl, nt, tl_ref, tr_ref, rowlim_ref, collim_ref, outlim_ref, sloc_ref,
           ts_ref, left_ref, mq_ref, rloc0_ref, rloc1_ref, lo_ref, hi_ref,
           out_ref, c_scr, x_scr, y_scr, kron_scr):
    i = pl.program_id(0)
    nb = pl.num_programs(0)
    depth = ts_ref.shape[-1]
    nq = ts_ref.shape[1]
    rows = lax.broadcasted_iota(jnp.int32, (depth, depth), 0)
    cols = lax.broadcasted_iota(jnp.int32, (depth, depth), 1)
    row_ok = rows < rowlim_ref[i]
    for q in range(nq):
        keep = row_ok & (cols < collim_ref[i * nq + q])
        c_scr[q] = jnp.where(keep, ts_ref[0, q], jnp.zeros_like(ts_ref[0, q]))

    nr = npl * nt
    rchunk = 32

    @pl.when(i == 0)
    def _():
        a = lax.broadcasted_iota(jnp.int32, (nr * YT, nr), 0)
        r = lax.broadcasted_iota(jnp.int32, (nr * YT, nr), 1)
        pick = jnp.where(a // YT == r, 1.0, 0.0).astype(mq_ref.dtype)
        rep = jnp.dot(pick, mq_ref[...], preferred_element_type=jnp.float32)
        ra = lax.broadcasted_iota(jnp.int32, rep.shape, 0)
        cb = lax.broadcasted_iota(jnp.int32, rep.shape, 1)
        kron_scr[...] = jnp.where(ra % YT == cb % YT, rep, 0.0).astype(kron_scr.dtype)

    for yb in range(0 if "nomix" in VARIANT else depth // (2 * YT)):
        ya, yc = 2 * yb * YT, (2 * yb + 1) * YT
        cy = jnp.concatenate(
            [c_scr[:, ya:ya + YT, :].reshape(nq * YT, depth),
             c_scr[:, yc:yc + YT, :].reshape(nq * YT, depth)], axis=1)
        for rc in range(nr // rchunk):
            k = kron_scr[rc * rchunk * YT:(rc + 1) * rchunk * YT, :]
            xy = jnp.dot(k, cy, preferred_element_type=jnp.float32)
            for half, y0 in enumerate((ya, yc)):
                x_scr[rc * rchunk:(rc + 1) * rchunk, y0:y0 + YT, :] = (
                    xy[:, half * depth:(half + 1) * depth]
                    .reshape(rchunk, YT, depth).astype(x_scr.dtype))

    def left_step(t, carry):
        lt = left_ref[tl_ref[t], 0]
        xs = jnp.concatenate([x_scr[t * npl + p] for p in range(npl)], axis=1)
        yt = jnp.dot(lt, xs, preferred_element_type=jnp.float32).astype(y_scr.dtype)
        for p in range(npl):
            y_scr[p, t] = yt[:, p * depth:(p + 1) * depth]
        return carry

    if "noleft" not in VARIANT:
        lax.fori_loop(0, nt, left_step, 0, unroll=UNROLL)

    def right_sum(p, src):
        def step(u, acc):
            ta, tb = 2 * u, 2 * u + 1
            lhs = jnp.concatenate([y_scr[p, ta], y_scr[p, tb]], axis=1)
            rhs = jnp.concatenate([src[tr_ref[ta], 0], src[tr_ref[tb], 0]], axis=0)
            return acc + jnp.dot(lhs, rhs, preferred_element_type=jnp.float32)
        acc = lax.fori_loop(0, nt // 2, step, jnp.zeros((depth, depth), jnp.float32),
                            unroll=UNROLL)
        keep = row_ok & (cols < outlim_ref[i * npl + p])
        out_ref[0, p] = jnp.where(keep, acc, 0.0).astype(out_ref.dtype)

    for p, rloc in enumerate(() if "noright" in VARIANT else (rloc0_ref, rloc1_ref)):
        j = i + sloc_ref[p]

        @pl.when(j < 0)
        def _():
            right_sum(p, lo_ref)

        @pl.when((j >= 0) & (j < nb))
        def _():
            right_sum(p, rloc)

        @pl.when(j >= nb)
        def _():
            right_sum(p, hi_ref)


def halos(cells, axis, dim, width):
    count = lax.axis_size(axis)
    ends = count - 1
    head = lax.slice_in_dim(cells, 0, width, axis=dim)
    tail = lax.slice_in_dim(cells, cells.shape[dim] - width, cells.shape[dim], axis=dim)
    lo = lax.ppermute(tail, axis, [(i, i + 1) for i in range(ends)])
    hi = lax.ppermute(head, axis, [(i + 1, i) for i in range(ends)])
    return lo, hi


def body(two_site, left_env, right_env, mpo_terms, term_left, term_right, shifts, block_sizes):
    blocks, nq, depth, _ = two_site.shape
    width = left_env.shape[0]
    nmpo = lax.axis_size("mpo")
    npl = nq // nmpo
    total = blocks * lax.axis_size("blk")
    first = lax.axis_index("blk") * blocks
    p_first = lax.axis_index("mpo") * npl

    local_terms = mpo_terms.shape[0]
    packed = jnp.concatenate(
        [mpo_terms.reshape(local_terms, nq * nq),
         term_left[:, None].astype(mpo_terms.dtype),
         term_right[:, None].astype(mpo_terms.dtype)], axis=1)
    packed = lax.all_gather(packed, "mpo", axis=0, tiled=True)
    nt = packed.shape[0]
    terms = packed[:, :nq * nq].reshape(nt, nq, nq)
    tl = packed[:, nq * nq].astype(jnp.int32)
    tr = packed[:, nq * nq + 1].astype(jnp.int32)

    rowlim, collim = sector_limits(block_sizes, shifts, first, blocks, total)
    outlim = lax.dynamic_slice_in_dim(collim, p_first, npl, axis=1)
    sloc = lax.dynamic_slice_in_dim(shifts, p_first, npl)

    mine = lax.dynamic_slice_in_dim(terms, p_first, npl, axis=1).reshape(nt * npl, nq)
    mq = jnp.repeat(mine, YT, axis=1)

    lo, hi = halos(right_env, "blk", 1, SH)

    return block_call(tl, tr, rowlim, collim.reshape(-1), outlim.reshape(-1), sloc,
                      two_site, left_env, mq, right_env, lo, hi)


def block_call(tl, tr, rowlim, collim, outlim, sloc, two_site, left_env, mq, right_env, lo, hi):
    blocks, nq, depth, _ = two_site.shape
    width = left_env.shape[0]
    npl = sloc.shape[0]
    nt = tl.shape[0]
    rblock = (width, 1, depth, depth)

    def rloc_map(p):
        def index(b, tl_r, tr_r, rl, cl, ol, sl):
            return (0, jnp.clip(b + sl[p], 0, blocks - 1), 0, 0)
        return index

    const4 = lambda b, *refs: (0, 0, 0, 0)
    grid_spec = pltpu.PrefetchScalarGridSpec(
        num_scalar_prefetch=6,
        grid=(blocks,),
        in_specs=[
            pl.BlockSpec((1, nq, depth, depth), lambda b, *refs: (b, 0, 0, 0)),
            pl.BlockSpec(rblock, lambda b, *refs: (0, b, 0, 0)),
            pl.BlockSpec(mq.shape, lambda b, *refs: (0, 0)),
            pl.BlockSpec(rblock, rloc_map(0)),
            pl.BlockSpec(rblock, rloc_map(1)),
            pl.BlockSpec(rblock, const4),
            pl.BlockSpec(rblock, const4),
        ],
        out_specs=pl.BlockSpec((1, npl, depth, depth), lambda b, *refs: (b, 0, 0, 0)),
        scratch_shapes=[
            pltpu.VMEM((nq, depth, depth), jnp.bfloat16),
            pltpu.VMEM((nt * npl, depth, depth), jnp.bfloat16),
            pltpu.VMEM((npl, nt, depth, depth), jnp.bfloat16),
            pltpu.VMEM((nt * npl * YT, nq * YT), jnp.bfloat16),
        ],
    )
    flops = 2 * blocks * (nt * npl * YT * nq * YT * depth + 2 * nt * npl * depth ** 3)
    return pl.pallas_call(
        functools.partial(kernel, npl, nt),
        out_shape=jax.ShapeDtypeStruct((blocks, npl, depth, depth), jnp.bfloat16),
        grid_spec=grid_spec,
        compiler_params=pltpu.CompilerParams(
            dimension_semantics=("arbitrary",), vmem_limit_bytes=60 * 1024 * 1024),
        cost_estimate=pl.CostEstimate(
            flops=flops, transcendentals=0,
            bytes_accessed=2 * (two_site.size + left_env.size + 3 * right_env.size)),
    )(tl, tr, rowlim, collim, outlim, sloc,
      two_site, left_env, mq, right_env, right_env, lo, hi)


def solution(mesh):
    return jax.shard_map(
        body,
        mesh=mesh,
        in_specs=(
            P("blk", None, None, None),
            P(None, "blk", None, None),
            P(None, "blk", None, None),
            P("mpo", None, None),
            P("mpo"),
            P("mpo"),
            P(),
            P(),
        ),
        out_specs=P("blk", "mpo", None, None),
        check_vma=False,
    )
```

```python
import functools

import jax
import jax.numpy as jnp
from jax import lax
from jax.experimental import pallas as pl
from jax.experimental.pallas import tpu as pltpu
from jax.sharding import PartitionSpec as P

SH = 1
YT = 16
UNROLL = 8
VARIANT = ""


def sector_limits(block_sizes, shifts, first, blocks, total):
    rows_left = first + jnp.arange(blocks, dtype=jnp.int32)
    right_index = rows_left[:, None] + shifts[None, :]
    inside = (right_index >= 0) & (right_index < total)
    size_left = block_sizes[rows_left]
    size_right = jnp.where(inside, block_sizes[jnp.clip(right_index, 0, total - 1)], 0)
    return size_left.astype(jnp.int32), size_right.astype(jnp.int32)


def kernel(npl, nt, tl_ref, tr_ref, rowlim_ref, collim_ref, outlim_ref, sloc_ref,
           ts_ref, left_ref, mq_ref, rloc0_ref, rloc1_ref, lo_ref, hi_ref,
           out_ref, c_scr, x_scr, y_scr, kron_scr):
    i = pl.program_id(0)
    nb = pl.num_programs(0)
    depth = ts_ref.shape[-1]
    nq = ts_ref.shape[1]
    rows = lax.broadcasted_iota(jnp.int32, (depth, depth), 0)
    cols = lax.broadcasted_iota(jnp.int32, (depth, depth), 1)
    row_ok = rows < rowlim_ref[i]
    for q in range(nq):
        keep = row_ok & (cols < collim_ref[i * nq + q])
        c_scr[q] = jnp.where(keep, ts_ref[0, q], jnp.zeros_like(ts_ref[0, q]))

    nr = npl * nt
    rchunk = 32

    @pl.when(i == 0)
    def _():
        a = lax.broadcasted_iota(jnp.int32, (nr * YT, nr), 0)
        r = lax.broadcasted_iota(jnp.int32, (nr * YT, nr), 1)
        pick = jnp.where(a // YT == r, 1.0, 0.0).astype(mq_ref.dtype)
        rep = jnp.dot(pick, mq_ref[...], preferred_element_type=jnp.float32)
        ra = lax.broadcasted_iota(jnp.int32, rep.shape, 0)
        cb = lax.broadcasted_iota(jnp.int32, rep.shape, 1)
        kron_scr[...] = jnp.where(ra % YT == cb % YT, rep, 0.0).astype(kron_scr.dtype)

    for yb in range(0 if "nomix" in VARIANT else depth // (2 * YT)):
        ya, yc = 2 * yb * YT, (2 * yb + 1) * YT
        cy = jnp.concatenate(
            [c_scr[:, ya:ya + YT, :].reshape(nq * YT, depth),
             c_scr[:, yc:yc + YT, :].reshape(nq * YT, depth)], axis=1)
        for rc in range(nr // rchunk):
            k = kron_scr[rc * rchunk * YT:(rc + 1) * rchunk * YT, :]
            xy = jnp.dot(k, cy, preferred_element_type=jnp.float32)
            for half, y0 in enumerate((ya, yc)):
                x_scr[rc * rchunk:(rc + 1) * rchunk, y0:y0 + YT, :] = (
                    xy[:, half * depth:(half + 1) * depth]
                    .reshape(rchunk, YT, depth).astype(x_scr.dtype))

    def left_step(t, carry):
        lt = left_ref[tl_ref[t], 0]
        xs = jnp.concatenate([x_scr[t * npl + p] for p in range(npl)], axis=1)
        yt = jnp.dot(lt, xs, preferred_element_type=jnp.float32).astype(y_scr.dtype)
        for p in range(npl):
            y_scr[p, t] = yt[:, p * depth:(p + 1) * depth]
        return carry

    if "noleft" not in VARIANT:
        lax.fori_loop(0, nt, left_step, 0, unroll=UNROLL)

    def right_sum(p, src):
        def step(u, acc):
            ta, tb = 2 * u, 2 * u + 1
            lhs = jnp.concatenate([y_scr[p, ta], y_scr[p, tb]], axis=1)
            rhs = jnp.concatenate([src[tr_ref[ta], 0], src[tr_ref[tb], 0]], axis=0)
            return acc + jnp.dot(lhs, rhs, preferred_element_type=jnp.float32)
        acc = lax.fori_loop(0, nt // 2, step, jnp.zeros((depth, depth), jnp.float32),
                            unroll=UNROLL)
        keep = row_ok & (cols < outlim_ref[i * npl + p])
        out_ref[0, p] = jnp.where(keep, acc, 0.0).astype(out_ref.dtype)

    for p, rloc in enumerate(() if "noright" in VARIANT else (rloc0_ref, rloc1_ref)):
        j = i + sloc_ref[p]

        @pl.when(j < 0)
        def _():
            right_sum(p, lo_ref)

        @pl.when((j >= 0) & (j < nb))
        def _():
            right_sum(p, rloc)

        @pl.when(j >= nb)
        def _():
            right_sum(p, hi_ref)


def gather_kernel(nm, x_ref, out_ref, send_sem, recv_sem):
    me = lax.axis_index("mpo")
    barrier = pltpu.get_barrier_semaphore()
    for d in range(1, nm):
        pl.semaphore_signal(barrier, inc=1, device_id={"mpo": lax.rem(me + d, nm)},
                            device_id_type=pl.DeviceIdType.MESH)
    pl.semaphore_wait(barrier, nm - 1)
    copies = []
    for d in range(1, nm):
        copy = pltpu.make_async_remote_copy(
            src_ref=x_ref,
            dst_ref=out_ref.at[me],
            send_sem=send_sem.at[d],
            recv_sem=recv_sem.at[d],
            device_id={"mpo": lax.rem(me + d, nm)},
            device_id_type=pl.DeviceIdType.MESH,
        )
        copy.start()
        copies.append(copy)
    out_ref[me] = x_ref[...]
    for copy in copies:
        copy.wait()


def gather_terms(packed):
    nm = lax.axis_size("mpo")
    return pl.pallas_call(
        functools.partial(gather_kernel, nm),
        out_shape=jax.ShapeDtypeStruct((nm,) + packed.shape, packed.dtype),
        in_specs=[pl.BlockSpec(memory_space=pltpu.VMEM)],
        out_specs=pl.BlockSpec(memory_space=pltpu.VMEM),
        scratch_shapes=[pltpu.SemaphoreType.DMA((nm,)), pltpu.SemaphoreType.DMA((nm,))],
        compiler_params=pltpu.CompilerParams(collective_id=0, has_side_effects=True),
    )(packed).reshape(nm * packed.shape[0], packed.shape[1])


def halos(cells, axis, dim, width):
    count = lax.axis_size(axis)
    ends = count - 1
    head = lax.slice_in_dim(cells, 0, width, axis=dim)
    tail = lax.slice_in_dim(cells, cells.shape[dim] - width, cells.shape[dim], axis=dim)
    lo = lax.ppermute(tail, axis, [(i, i + 1) for i in range(ends)])
    hi = lax.ppermute(head, axis, [(i + 1, i) for i in range(ends)])
    return lo, hi


def body(two_site, left_env, right_env, mpo_terms, term_left, term_right, shifts, block_sizes):
    blocks, nq, depth, _ = two_site.shape
    width = left_env.shape[0]
    nmpo = lax.axis_size("mpo")
    npl = nq // nmpo
    total = blocks * lax.axis_size("blk")
    first = lax.axis_index("blk") * blocks
    p_first = lax.axis_index("mpo") * npl

    local_terms = mpo_terms.shape[0]
    packed = jnp.concatenate(
        [mpo_terms.reshape(local_terms, nq * nq),
         term_left[:, None].astype(mpo_terms.dtype),
         term_right[:, None].astype(mpo_terms.dtype)], axis=1).astype(jnp.float32)
    packed = gather_terms(packed)
    nt = packed.shape[0]
    terms = packed[:, :nq * nq].reshape(nt, nq, nq).astype(mpo_terms.dtype)
    tl = packed[:, nq * nq].astype(jnp.int32)
    tr = packed[:, nq * nq + 1].astype(jnp.int32)

    rowlim, collim = sector_limits(block_sizes, shifts, first, blocks, total)
    outlim = lax.dynamic_slice_in_dim(collim, p_first, npl, axis=1)
    sloc = lax.dynamic_slice_in_dim(shifts, p_first, npl)

    mine = lax.dynamic_slice_in_dim(terms, p_first, npl, axis=1).reshape(nt * npl, nq)
    mq = jnp.repeat(mine, YT, axis=1)

    lo, hi = halos(right_env, "blk", 1, SH)

    return block_call(tl, tr, rowlim, collim.reshape(-1), outlim.reshape(-1), sloc,
                      two_site, left_env, mq, right_env, lo, hi)


def block_call(tl, tr, rowlim, collim, outlim, sloc, two_site, left_env, mq, right_env, lo, hi):
    blocks, nq, depth, _ = two_site.shape
    width = left_env.shape[0]
    npl = sloc.shape[0]
    nt = tl.shape[0]
    rblock = (width, 1, depth, depth)

    def rloc_map(p):
        def index(b, tl_r, tr_r, rl, cl, ol, sl):
            return (0, jnp.clip(b + sl[p], 0, blocks - 1), 0, 0)
        return index

    const4 = lambda b, *refs: (0, 0, 0, 0)
    grid_spec = pltpu.PrefetchScalarGridSpec(
        num_scalar_prefetch=6,
        grid=(blocks,),
        in_specs=[
            pl.BlockSpec((1, nq, depth, depth), lambda b, *refs: (b, 0, 0, 0)),
            pl.BlockSpec(rblock, lambda b, *refs: (0, b, 0, 0)),
            pl.BlockSpec(mq.shape, lambda b, *refs: (0, 0)),
            pl.BlockSpec(rblock, rloc_map(0)),
            pl.BlockSpec(rblock, rloc_map(1)),
            pl.BlockSpec(rblock, const4),
            pl.BlockSpec(rblock, const4),
        ],
        out_specs=pl.BlockSpec((1, npl, depth, depth), lambda b, *refs: (b, 0, 0, 0)),
        scratch_shapes=[
            pltpu.VMEM((nq, depth, depth), jnp.bfloat16),
            pltpu.VMEM((nt * npl, depth, depth), jnp.bfloat16),
            pltpu.VMEM((npl, nt, depth, depth), jnp.bfloat16),
            pltpu.VMEM((nt * npl * YT, nq * YT), jnp.bfloat16),
        ],
    )
    flops = 2 * blocks * (nt * npl * YT * nq * YT * depth + 2 * nt * npl * depth ** 3)
    return pl.pallas_call(
        functools.partial(kernel, npl, nt),
        out_shape=jax.ShapeDtypeStruct((blocks, npl, depth, depth), jnp.bfloat16),
        grid_spec=grid_spec,
        compiler_params=pltpu.CompilerParams(
            dimension_semantics=("arbitrary",), vmem_limit_bytes=60 * 1024 * 1024),
        cost_estimate=pl.CostEstimate(
            flops=flops, transcendentals=0,
            bytes_accessed=2 * (two_site.size + left_env.size + 3 * right_env.size)),
    )(tl, tr, rowlim, collim, outlim, sloc,
      two_site, left_env, mq, right_env, right_env, lo, hi)


def solution(mesh):
    return jax.shard_map(
        body,
        mesh=mesh,
        in_specs=(
            P("blk", None, None, None),
            P(None, "blk", None, None),
            P(None, "blk", None, None),
            P("mpo", None, None),
            P("mpo"),
            P("mpo"),
            P(),
            P(),
        ),
        out_specs=P("blk", "mpo", None, None),
        check_vma=False,
    )
```

```python
import functools

import jax
import jax.numpy as jnp
from jax import lax
from jax.experimental import pallas as pl
from jax.experimental.pallas import tpu as pltpu
from jax.sharding import PartitionSpec as P

SH = 1
YT = 16
UNROLL = 32
VARIANT = ""
RG = 4
RCHUNK = 64


def sector_limits(block_sizes, shifts, first, blocks, total):
    rows_left = first + jnp.arange(blocks, dtype=jnp.int32)
    right_index = rows_left[:, None] + shifts[None, :]
    inside = (right_index >= 0) & (right_index < total)
    size_left = block_sizes[rows_left]
    size_right = jnp.where(inside, block_sizes[jnp.clip(right_index, 0, total - 1)], 0)
    return size_left.astype(jnp.int32), size_right.astype(jnp.int32)


def kernel(npl, nt, tl_ref, tr_ref, rowlim_ref, collim_ref, outlim_ref, sloc_ref,
           ts_ref, left_ref, mq_ref, rloc0_ref, rloc1_ref, lo_ref, hi_ref,
           out_ref, c_scr, x_scr, y_scr, kron_scr):
    i = pl.program_id(0)
    nb = pl.num_programs(0)
    depth = ts_ref.shape[-1]
    nq = ts_ref.shape[1]
    rows = lax.broadcasted_iota(jnp.int32, (depth, depth), 0)
    cols = lax.broadcasted_iota(jnp.int32, (depth, depth), 1)
    row_ok = rows < rowlim_ref[i]
    for q in range(nq):
        keep = row_ok & (cols < collim_ref[i * nq + q])
        c_scr[q] = jnp.where(keep, ts_ref[0, q], jnp.zeros_like(ts_ref[0, q]))

    nr = npl * nt
    rchunk = RCHUNK

    @pl.when(i == 0)
    def _():
        a = lax.broadcasted_iota(jnp.int32, (nr * YT, nr), 0)
        r = lax.broadcasted_iota(jnp.int32, (nr * YT, nr), 1)
        pick = jnp.where(a // YT == r, 1.0, 0.0).astype(mq_ref.dtype)
        rep = jnp.dot(pick, mq_ref[...], preferred_element_type=jnp.float32)
        ra = lax.broadcasted_iota(jnp.int32, rep.shape, 0)
        cb = lax.broadcasted_iota(jnp.int32, rep.shape, 1)
        kron_scr[...] = jnp.where(ra % YT == cb % YT, rep, 0.0).astype(kron_scr.dtype)

    for yb in range(0 if "nomix" in VARIANT else depth // (2 * YT)):
        ya, yc = 2 * yb * YT, (2 * yb + 1) * YT
        cy = jnp.concatenate(
            [c_scr[:, ya:ya + YT, :].reshape(nq * YT, depth),
             c_scr[:, yc:yc + YT, :].reshape(nq * YT, depth)], axis=1)
        for rc in range(nr // rchunk):
            k = kron_scr[rc * rchunk * YT:(rc + 1) * rchunk * YT, :]
            xy = jnp.dot(k, cy, preferred_element_type=jnp.float32)
            for half, y0 in enumerate((ya, yc)):
                x_scr[rc * rchunk:(rc + 1) * rchunk, y0:y0 + YT, :] = (
                    xy[:, half * depth:(half + 1) * depth]
                    .reshape(rchunk, YT, depth).astype(x_scr.dtype))

    def left_step(t, carry):
        lt = left_ref[tl_ref[t], 0]
        xs = jnp.concatenate([x_scr[t * npl + p] for p in range(npl)], axis=1)
        yt = jnp.dot(lt, xs, preferred_element_type=jnp.float32).astype(y_scr.dtype)
        for p in range(npl):
            y_scr[p, t] = yt[:, p * depth:(p + 1) * depth]
        return carry

    if "noleft" not in VARIANT:
        lax.fori_loop(0, nt, left_step, 0, unroll=UNROLL)

    def right_sum(p, src):
        def step(u, acc):
            ts_ = [RG * u + g for g in range(RG)]
            lhs = jnp.concatenate([y_scr[p, t] for t in ts_], axis=1)
            rhs = jnp.concatenate([src[tr_ref[t], 0] for t in ts_], axis=0)
            return acc + jnp.dot(lhs, rhs, preferred_element_type=jnp.float32)
        acc = lax.fori_loop(0, nt // RG, step, jnp.zeros((depth, depth), jnp.float32),
                            unroll=max(1, UNROLL * 2 // RG))
        keep = row_ok & (cols < outlim_ref[i * npl + p])
        out_ref[0, p] = jnp.where(keep, acc, 0.0).astype(out_ref.dtype)

    for p, rloc in enumerate(() if "noright" in VARIANT else (rloc0_ref, rloc1_ref)):
        j = i + sloc_ref[p]

        @pl.when(j < 0)
        def _():
            right_sum(p, lo_ref)

        @pl.when((j >= 0) & (j < nb))
        def _():
            right_sum(p, rloc)

        @pl.when(j >= nb)
        def _():
            right_sum(p, hi_ref)


def gather_kernel(nm, x_ref, out_ref, send_sem, recv_sem):
    me = lax.axis_index("mpo")
    barrier = pltpu.get_barrier_semaphore()
    for d in range(1, nm):
        pl.semaphore_signal(barrier, inc=1, device_id={"mpo": lax.rem(me + d, nm)},
                            device_id_type=pl.DeviceIdType.MESH)
    pl.semaphore_wait(barrier, nm - 1)
    copies = []
    for d in range(1, nm):
        copy = pltpu.make_async_remote_copy(
            src_ref=x_ref,
            dst_ref=out_ref.at[me],
            send_sem=send_sem.at[d],
            recv_sem=recv_sem.at[d],
            device_id={"mpo": lax.rem(me + d, nm)},
            device_id_type=pl.DeviceIdType.MESH,
        )
        copy.start()
        copies.append(copy)
    out_ref[me] = x_ref[...]
    for copy in copies:
        copy.wait()


def gather_terms(packed):
    nm = lax.axis_size("mpo")
    return pl.pallas_call(
        functools.partial(gather_kernel, nm),
        out_shape=jax.ShapeDtypeStruct((nm,) + packed.shape, packed.dtype),
        in_specs=[pl.BlockSpec(memory_space=pltpu.VMEM)],
        out_specs=pl.BlockSpec(memory_space=pltpu.VMEM),
        scratch_shapes=[pltpu.SemaphoreType.DMA((nm,)), pltpu.SemaphoreType.DMA((nm,))],
        compiler_params=pltpu.CompilerParams(collective_id=0, has_side_effects=True),
    )(packed).reshape(nm * packed.shape[0], packed.shape[1])


def halos(cells, axis, dim, width):
    count = lax.axis_size(axis)
    ends = count - 1
    head = lax.slice_in_dim(cells, 0, width, axis=dim)
    tail = lax.slice_in_dim(cells, cells.shape[dim] - width, cells.shape[dim], axis=dim)
    lo = lax.ppermute(tail, axis, [(i, i + 1) for i in range(ends)])
    hi = lax.ppermute(head, axis, [(i + 1, i) for i in range(ends)])
    return lo, hi


def body(two_site, left_env, right_env, mpo_terms, term_left, term_right, shifts, block_sizes):
    blocks, nq, depth, _ = two_site.shape
    width = left_env.shape[0]
    nmpo = lax.axis_size("mpo")
    npl = nq // nmpo
    total = blocks * lax.axis_size("blk")
    first = lax.axis_index("blk") * blocks
    p_first = lax.axis_index("mpo") * npl

    local_terms = mpo_terms.shape[0]
    packed = jnp.concatenate(
        [mpo_terms.reshape(local_terms, nq * nq),
         term_left[:, None].astype(mpo_terms.dtype),
         term_right[:, None].astype(mpo_terms.dtype)], axis=1).astype(jnp.float32)
    packed = gather_terms(packed)
    nt = packed.shape[0]
    terms = packed[:, :nq * nq].reshape(nt, nq, nq).astype(mpo_terms.dtype)
    tl = packed[:, nq * nq].astype(jnp.int32)
    tr = packed[:, nq * nq + 1].astype(jnp.int32)

    rowlim, collim = sector_limits(block_sizes, shifts, first, blocks, total)
    outlim = lax.dynamic_slice_in_dim(collim, p_first, npl, axis=1)
    sloc = lax.dynamic_slice_in_dim(shifts, p_first, npl)

    mine = lax.dynamic_slice_in_dim(terms, p_first, npl, axis=1).reshape(nt * npl, nq)
    mq = jnp.repeat(mine, YT, axis=1)

    lo, hi = halos(right_env, "blk", 1, SH)

    return block_call(tl, tr, rowlim, collim.reshape(-1), outlim.reshape(-1), sloc,
                      two_site, left_env, mq, right_env, lo, hi)


def block_call(tl, tr, rowlim, collim, outlim, sloc, two_site, left_env, mq, right_env, lo, hi):
    blocks, nq, depth, _ = two_site.shape
    width = left_env.shape[0]
    npl = sloc.shape[0]
    nt = tl.shape[0]
    rblock = (width, 1, depth, depth)

    def rloc_map(p):
        def index(b, tl_r, tr_r, rl, cl, ol, sl):
            return (0, jnp.clip(b + sl[p], 0, blocks - 1), 0, 0)
        return index

    const4 = lambda b, *refs: (0, 0, 0, 0)
    grid_spec = pltpu.PrefetchScalarGridSpec(
        num_scalar_prefetch=6,
        grid=(blocks,),
        in_specs=[
            pl.BlockSpec((1, nq, depth, depth), lambda b, *refs: (b, 0, 0, 0)),
            pl.BlockSpec(rblock, lambda b, *refs: (0, b, 0, 0)),
            pl.BlockSpec(mq.shape, lambda b, *refs: (0, 0)),
            pl.BlockSpec(rblock, rloc_map(0)),
            pl.BlockSpec(rblock, rloc_map(1)),
            pl.BlockSpec(rblock, const4),
            pl.BlockSpec(rblock, const4),
        ],
        out_specs=pl.BlockSpec((1, npl, depth, depth), lambda b, *refs: (b, 0, 0, 0)),
        scratch_shapes=[
            pltpu.VMEM((nq, depth, depth), jnp.bfloat16),
            pltpu.VMEM((nt * npl, depth, depth), jnp.bfloat16),
            pltpu.VMEM((npl, nt, depth, depth), jnp.bfloat16),
            pltpu.VMEM((nt * npl * YT, nq * YT), jnp.bfloat16),
        ],
    )
    flops = 2 * blocks * (nt * npl * YT * nq * YT * depth + 2 * nt * npl * depth ** 3)
    return pl.pallas_call(
        functools.partial(kernel, npl, nt),
        out_shape=jax.ShapeDtypeStruct((blocks, npl, depth, depth), jnp.bfloat16),
        grid_spec=grid_spec,
        compiler_params=pltpu.CompilerParams(
            dimension_semantics=("arbitrary",), vmem_limit_bytes=60 * 1024 * 1024),
        cost_estimate=pl.CostEstimate(
            flops=flops, transcendentals=0,
            bytes_accessed=2 * (two_site.size + left_env.size + 3 * right_env.size)),
    )(tl, tr, rowlim, collim, outlim, sloc,
      two_site, left_env, mq, right_env, right_env, lo, hi)


def solution(mesh):
    return jax.shard_map(
        body,
        mesh=mesh,
        in_specs=(
            P("blk", None, None, None),
            P(None, "blk", None, None),
            P(None, "blk", None, None),
            P("mpo", None, None),
            P("mpo"),
            P("mpo"),
            P(),
            P(),
        ),
        out_specs=P("blk", "mpo", None, None),
        check_vma=False,
    )
```

```python
import functools

import jax
import jax.numpy as jnp
from jax import lax
from jax.experimental import pallas as pl
from jax.experimental.pallas import tpu as pltpu
from jax.sharding import PartitionSpec as P

SH = 1
YT = 16
UNROLL = 32
RUNROLL = 16
VARIANT = ""
RG = 4
RCHUNK = 64


def sector_limits(block_sizes, shifts, first, blocks, total):
    rows_left = first + jnp.arange(blocks, dtype=jnp.int32)
    right_index = rows_left[:, None] + shifts[None, :]
    inside = (right_index >= 0) & (right_index < total)
    size_left = block_sizes[rows_left]
    size_right = jnp.where(inside, block_sizes[jnp.clip(right_index, 0, total - 1)], 0)
    return size_left.astype(jnp.int32), size_right.astype(jnp.int32)


def kernel(npl, nt, base, stride, nb, halo, *refs):
    (tl_ref, tr_ref, rowlim_ref, collim_ref, outlim_ref, sloc_ref,
     ts_ref, left_ref, mq_ref, rloc0_ref, rloc1_ref) = refs[:11]
    if halo:
        lo_ref, hi_ref = refs[11:13]
        refs = refs[14:]
    else:
        refs = refs[11:]
    out_ref, c_scr, x_scr, y_scr, kron_scr = refs
    first_step = pl.program_id(0) == 0
    i = base + pl.program_id(0) * stride
    depth = ts_ref.shape[-1]
    nq = ts_ref.shape[1]
    rows = lax.broadcasted_iota(jnp.int32, (depth, depth), 0)
    cols = lax.broadcasted_iota(jnp.int32, (depth, depth), 1)
    row_ok = rows < rowlim_ref[i]
    for q in range(nq):
        keep = row_ok & (cols < collim_ref[i * nq + q])
        c_scr[q] = jnp.where(keep, ts_ref[0, q], jnp.zeros_like(ts_ref[0, q]))

    nr = npl * nt
    rchunk = RCHUNK

    @pl.when(first_step)
    def _():
        a = lax.broadcasted_iota(jnp.int32, (nr * YT, nr), 0)
        r = lax.broadcasted_iota(jnp.int32, (nr * YT, nr), 1)
        pick = jnp.where(a // YT == r, 1.0, 0.0).astype(mq_ref.dtype)
        rep = jnp.dot(pick, mq_ref[...], preferred_element_type=jnp.float32)
        ra = lax.broadcasted_iota(jnp.int32, rep.shape, 0)
        cb = lax.broadcasted_iota(jnp.int32, rep.shape, 1)
        kron_scr[...] = jnp.where(ra % YT == cb % YT, rep, 0.0).astype(kron_scr.dtype)

    for yb in range(0 if "nomix" in VARIANT else depth // (2 * YT)):
        ya, yc = 2 * yb * YT, (2 * yb + 1) * YT
        cy = jnp.concatenate(
            [c_scr[:, ya:ya + YT, :].reshape(nq * YT, depth),
             c_scr[:, yc:yc + YT, :].reshape(nq * YT, depth)], axis=1)
        for rc in range(nr // rchunk):
            k = kron_scr[rc * rchunk * YT:(rc + 1) * rchunk * YT, :]
            xy = jnp.dot(k, cy, preferred_element_type=jnp.float32)
            for half, y0 in enumerate((ya, yc)):
                x_scr[rc * rchunk:(rc + 1) * rchunk, y0:y0 + YT, :] = (
                    xy[:, half * depth:(half + 1) * depth]
                    .reshape(rchunk, YT, depth).astype(x_scr.dtype))

    def left_step(t, carry):
        lt = left_ref[tl_ref[t], 0]
        xs = jnp.concatenate([x_scr[t * npl + p] for p in range(npl)], axis=1)
        yt = jnp.dot(lt, xs, preferred_element_type=jnp.float32).astype(y_scr.dtype)
        for p in range(npl):
            y_scr[p, t] = yt[:, p * depth:(p + 1) * depth]
        return carry

    if "noleft" not in VARIANT:
        lax.fori_loop(0, nt, left_step, 0, unroll=UNROLL)

    def right_sum(p, src):
        def step(u, acc):
            ts_ = [RG * u + g for g in range(RG)]
            lhs = jnp.concatenate([y_scr[p, t] for t in ts_], axis=1)
            rhs = jnp.concatenate([src[tr_ref[t], 0] for t in ts_], axis=0)
            return acc + jnp.dot(lhs, rhs, preferred_element_type=jnp.float32)
        acc = lax.fori_loop(0, nt // RG, step, jnp.zeros((depth, depth), jnp.float32),
                            unroll=RUNROLL)
        keep = row_ok & (cols < outlim_ref[i * npl + p])
        out_ref[0, p] = jnp.where(keep, acc, 0.0).astype(out_ref.dtype)

    for p, rloc in enumerate(() if "noright" in VARIANT else (rloc0_ref, rloc1_ref)):
        if not halo:
            right_sum(p, rloc)
            continue
        j = i + sloc_ref[p]

        @pl.when(j < 0)
        def _():
            right_sum(p, lo_ref)

        @pl.when((j >= 0) & (j < nb))
        def _():
            right_sum(p, rloc)

        @pl.when(j >= nb)
        def _():
            right_sum(p, hi_ref)


def gather_kernel(nm, x_ref, out_ref, send_sem, recv_sem):
    me = lax.axis_index("mpo")
    barrier = pltpu.get_barrier_semaphore()
    for d in range(1, nm):
        pl.semaphore_signal(barrier, inc=1, device_id={"mpo": lax.rem(me + d, nm)},
                            device_id_type=pl.DeviceIdType.MESH)
    pl.semaphore_wait(barrier, nm - 1)
    copies = []
    for d in range(1, nm):
        copy = pltpu.make_async_remote_copy(
            src_ref=x_ref,
            dst_ref=out_ref.at[me],
            send_sem=send_sem.at[d],
            recv_sem=recv_sem.at[d],
            device_id={"mpo": lax.rem(me + d, nm)},
            device_id_type=pl.DeviceIdType.MESH,
        )
        copy.start()
        copies.append(copy)
    out_ref[me] = x_ref[...]
    for copy in copies:
        copy.wait()


def gather_terms(packed):
    nm = lax.axis_size("mpo")
    return pl.pallas_call(
        functools.partial(gather_kernel, nm),
        out_shape=jax.ShapeDtypeStruct((nm,) + packed.shape, packed.dtype),
        in_specs=[pl.BlockSpec(memory_space=pltpu.VMEM)],
        out_specs=pl.BlockSpec(memory_space=pltpu.VMEM),
        scratch_shapes=[pltpu.SemaphoreType.DMA((nm,)), pltpu.SemaphoreType.DMA((nm,))],
        compiler_params=pltpu.CompilerParams(collective_id=0, has_side_effects=True),
    )(packed).reshape(nm * packed.shape[0], packed.shape[1])


def halos(cells, axis, dim, width):
    count = lax.axis_size(axis)
    ends = count - 1
    head = lax.slice_in_dim(cells, 0, width, axis=dim)
    tail = lax.slice_in_dim(cells, cells.shape[dim] - width, cells.shape[dim], axis=dim)
    lo = lax.ppermute(tail, axis, [(i, i + 1) for i in range(ends)])
    hi = lax.ppermute(head, axis, [(i + 1, i) for i in range(ends)])
    return lo, hi


def body(two_site, left_env, right_env, mpo_terms, term_left, term_right, shifts, block_sizes):
    blocks, nq, depth, _ = two_site.shape
    width = left_env.shape[0]
    nmpo = lax.axis_size("mpo")
    npl = nq // nmpo
    total = blocks * lax.axis_size("blk")
    first = lax.axis_index("blk") * blocks
    p_first = lax.axis_index("mpo") * npl

    local_terms = mpo_terms.shape[0]
    packed = jnp.concatenate(
        [mpo_terms.reshape(local_terms, nq * nq),
         term_left[:, None].astype(mpo_terms.dtype),
         term_right[:, None].astype(mpo_terms.dtype)], axis=1).astype(jnp.float32)
    packed = gather_terms(packed)
    nt = packed.shape[0]
    terms = packed[:, :nq * nq].reshape(nt, nq, nq).astype(mpo_terms.dtype)
    tl = packed[:, nq * nq].astype(jnp.int32)
    tr = packed[:, nq * nq + 1].astype(jnp.int32)

    rowlim, collim = sector_limits(block_sizes, shifts, first, blocks, total)
    outlim = lax.dynamic_slice_in_dim(collim, p_first, npl, axis=1)
    sloc = lax.dynamic_slice_in_dim(shifts, p_first, npl)

    mine = lax.dynamic_slice_in_dim(terms, p_first, npl, axis=1).reshape(nt * npl, nq)
    mq = jnp.repeat(mine, YT, axis=1)

    lo, hi = halos(right_env, "blk", 1, SH)

    scalars = (tl, tr, rowlim, collim.reshape(-1), outlim.reshape(-1), sloc)
    inner = block_call(*scalars, two_site, left_env, mq, right_env, None, None, None)
    return block_call(*scalars, two_site, left_env, mq, right_env, lo, hi, inner)


def block_call(tl, tr, rowlim, collim, outlim, sloc, two_site, left_env, mq, right_env,
               lo, hi, prev):
    blocks, nq, depth, _ = two_site.shape
    halo = prev is not None
    if halo:
        base, stride, steps = 0, blocks - 1, 2
    else:
        base, stride, steps = 1, 1, blocks - 2
    width = left_env.shape[0]
    npl = sloc.shape[0]
    nt = tl.shape[0]
    rblock = (width, 1, depth, depth)

    def rloc_map(p):
        def index(b, tl_r, tr_r, rl, cl, ol, sl):
            return (0, jnp.clip(base + b * stride + sl[p], 0, blocks - 1), 0, 0)
        return index

    const4 = lambda b, *refs: (0, 0, 0, 0)
    in_specs = [
        pl.BlockSpec((1, nq, depth, depth), lambda b, *refs: (base + b * stride, 0, 0, 0)),
        pl.BlockSpec(rblock, lambda b, *refs: (0, base + b * stride, 0, 0)),
        pl.BlockSpec(mq.shape, lambda b, *refs: (0, 0)),
        pl.BlockSpec(rblock, rloc_map(0)),
        pl.BlockSpec(rblock, rloc_map(1)),
    ]
    operands = [two_site, left_env, mq, right_env, right_env]
    aliases = {}
    if halo:
        in_specs += [pl.BlockSpec(rblock, const4), pl.BlockSpec(rblock, const4),
                     pl.BlockSpec(memory_space=pl.ANY)]
        operands += [lo, hi, prev]
        aliases = {6 + len(operands) - 1: 0}
    grid_spec = pltpu.PrefetchScalarGridSpec(
        num_scalar_prefetch=6,
        grid=(steps,),
        in_specs=in_specs,
        out_specs=pl.BlockSpec((1, npl, depth, depth),
                               lambda b, *refs: (base + b * stride, 0, 0, 0)),
        scratch_shapes=[
            pltpu.VMEM((nq, depth, depth), jnp.bfloat16),
            pltpu.VMEM((nt * npl, depth, depth), jnp.bfloat16),
            pltpu.VMEM((npl, nt, depth, depth), jnp.bfloat16),
            pltpu.VMEM((nt * npl * YT, nq * YT), jnp.bfloat16),
        ],
    )
    flops = 2 * steps * (nt * npl * YT * nq * YT * depth + 2 * nt * npl * depth ** 3)
    return pl.pallas_call(
        functools.partial(kernel, npl, nt, base, stride, blocks, halo),
        out_shape=jax.ShapeDtypeStruct((blocks, npl, depth, depth), jnp.bfloat16),
        grid_spec=grid_spec,
        compiler_params=pltpu.CompilerParams(
            dimension_semantics=("arbitrary",), vmem_limit_bytes=60 * 1024 * 1024),
        cost_estimate=pl.CostEstimate(
            flops=flops, transcendentals=0,
            bytes_accessed=2 * steps * (two_site.size + left_env.size + 3 * right_env.size)
            // blocks),
        input_output_aliases=aliases,
    )(tl, tr, rowlim, collim, outlim, sloc, *operands)


def solution(mesh):
    return jax.shard_map(
        body,
        mesh=mesh,
        in_specs=(
            P("blk", None, None, None),
            P(None, "blk", None, None),
            P(None, "blk", None, None),
            P("mpo", None, None),
            P("mpo"),
            P("mpo"),
            P(),
            P(),
        ),
        out_specs=P("blk", "mpo", None, None),
        check_vma=False,
    )
```

```python
import functools

import jax
import jax.numpy as jnp
from jax import lax
from jax.experimental import pallas as pl
from jax.experimental.pallas import tpu as pltpu
from jax.sharding import PartitionSpec as P

SH = 1
YT = 16
UNROLL = 32
RUNROLL = 16
VARIANT = ""
RG = 4
RCHUNK = 64


def kernel(npl, nt, base, stride, nb, total, halo, *refs):
    (tl_ref, tr_ref, bs_ref, sh_ref, ids_ref,
     ts_ref, left_ref, mq_ref, rloc0_ref, rloc1_ref) = refs[:10]
    if halo:
        lo_ref, hi_ref = refs[10:12]
        refs = refs[13:]
    else:
        refs = refs[10:]
    out_ref, c_scr, x_scr, y_scr, kron_scr = refs
    first_step = pl.program_id(0) == 0
    i = base + pl.program_id(0) * stride
    gi = ids_ref[0] + i

    def size_at(shift):
        j = gi + shift
        inside = (j >= 0) & (j < total)
        return jnp.where(inside, bs_ref[jnp.clip(j, 0, total - 1)], 0)

    sloc = [sh_ref[ids_ref[1] + p] for p in range(npl)]
    depth = ts_ref.shape[-1]
    nq = ts_ref.shape[1]
    rows = lax.broadcasted_iota(jnp.int32, (depth, depth), 0)
    cols = lax.broadcasted_iota(jnp.int32, (depth, depth), 1)
    row_ok = rows < bs_ref[gi]
    for q in range(nq):
        keep = row_ok & (cols < size_at(sh_ref[q]))
        c_scr[q] = jnp.where(keep, ts_ref[0, q], jnp.zeros_like(ts_ref[0, q]))

    nr = npl * nt
    rchunk = RCHUNK

    @pl.when(first_step)
    def _():
        a = lax.broadcasted_iota(jnp.int32, (nr * YT, nr), 0)
        r = lax.broadcasted_iota(jnp.int32, (nr * YT, nr), 1)
        pick = jnp.where(a // YT == r, 1.0, 0.0).astype(mq_ref.dtype)
        rep = jnp.dot(pick, mq_ref[...], preferred_element_type=jnp.float32)
        ra = lax.broadcasted_iota(jnp.int32, rep.shape, 0)
        cb = lax.broadcasted_iota(jnp.int32, rep.shape, 1)
        kron_scr[...] = jnp.where(ra % YT == cb % YT, rep, 0.0).astype(kron_scr.dtype)

    for yb in range(0 if "nomix" in VARIANT else depth // (2 * YT)):
        ya, yc = 2 * yb * YT, (2 * yb + 1) * YT
        cy = jnp.concatenate(
            [c_scr[:, ya:ya + YT, :].reshape(nq * YT, depth),
             c_scr[:, yc:yc + YT, :].reshape(nq * YT, depth)], axis=1)
        for rc in range(nr // rchunk):
            k = kron_scr[rc * rchunk * YT:(rc + 1) * rchunk * YT, :]
            xy = jnp.dot(k, cy, preferred_element_type=jnp.float32)
            for half, y0 in enumerate((ya, yc)):
                x_scr[rc * rchunk:(rc + 1) * rchunk, y0:y0 + YT, :] = (
                    xy[:, half * depth:(half + 1) * depth]
                    .reshape(rchunk, YT, depth).astype(x_scr.dtype))

    def left_step(t, carry):
        lt = left_ref[tl_ref[t], 0]
        xs = jnp.concatenate([x_scr[t * npl + p] for p in range(npl)], axis=1)
        yt = jnp.dot(lt, xs, preferred_element_type=jnp.float32).astype(y_scr.dtype)
        for p in range(npl):
            y_scr[p, t] = yt[:, p * depth:(p + 1) * depth]
        return carry

    if "noleft" not in VARIANT:
        lax.fori_loop(0, nt, left_step, 0, unroll=UNROLL)

    def right_sum(p, src):
        def step(u, acc):
            ts_ = [RG * u + g for g in range(RG)]
            lhs = jnp.concatenate([y_scr[p, t] for t in ts_], axis=1)
            rhs = jnp.concatenate([src[tr_ref[t], 0] for t in ts_], axis=0)
            return acc + jnp.dot(lhs, rhs, preferred_element_type=jnp.float32)
        acc = lax.fori_loop(0, nt // RG, step, jnp.zeros((depth, depth), jnp.float32),
                            unroll=RUNROLL)
        keep = row_ok & (cols < size_at(sloc[p]))
        out_ref[0, p] = jnp.where(keep, acc, 0.0).astype(out_ref.dtype)

    for p, rloc in enumerate(() if "noright" in VARIANT else (rloc0_ref, rloc1_ref)):
        if not halo:
            right_sum(p, rloc)
            continue
        j = i + sloc[p]

        @pl.when(j < 0)
        def _():
            right_sum(p, lo_ref)

        @pl.when((j >= 0) & (j < nb))
        def _():
            right_sum(p, rloc)

        @pl.when(j >= nb)
        def _():
            right_sum(p, hi_ref)


def gather_kernel(nm, x_ref, out_ref, send_sem, recv_sem):
    me = lax.axis_index("mpo")
    barrier = pltpu.get_barrier_semaphore()
    for d in range(1, nm):
        pl.semaphore_signal(barrier, inc=1, device_id={"mpo": lax.rem(me + d, nm)},
                            device_id_type=pl.DeviceIdType.MESH)
    pl.semaphore_wait(barrier, nm - 1)
    copies = []
    for d in range(1, nm):
        copy = pltpu.make_async_remote_copy(
            src_ref=x_ref,
            dst_ref=out_ref.at[me],
            send_sem=send_sem.at[d],
            recv_sem=recv_sem.at[d],
            device_id={"mpo": lax.rem(me + d, nm)},
            device_id_type=pl.DeviceIdType.MESH,
        )
        copy.start()
        copies.append(copy)
    out_ref[me] = x_ref[...]
    for copy in copies:
        copy.wait()


def gather_terms(packed):
    nm = lax.axis_size("mpo")
    return pl.pallas_call(
        functools.partial(gather_kernel, nm),
        out_shape=jax.ShapeDtypeStruct((nm,) + packed.shape, packed.dtype),
        in_specs=[pl.BlockSpec(memory_space=pltpu.VMEM)],
        out_specs=pl.BlockSpec(memory_space=pltpu.VMEM),
        scratch_shapes=[pltpu.SemaphoreType.DMA((nm,)), pltpu.SemaphoreType.DMA((nm,))],
        compiler_params=pltpu.CompilerParams(collective_id=0, has_side_effects=True),
    )(packed).reshape(nm * packed.shape[0], packed.shape[1])


def halos(cells, axis, dim, width):
    count = lax.axis_size(axis)
    ends = count - 1
    head = lax.slice_in_dim(cells, 0, width, axis=dim)
    tail = lax.slice_in_dim(cells, cells.shape[dim] - width, cells.shape[dim], axis=dim)
    lo = lax.ppermute(tail, axis, [(i, i + 1) for i in range(ends)])
    hi = lax.ppermute(head, axis, [(i + 1, i) for i in range(ends)])
    return lo, hi


def body(two_site, left_env, right_env, mpo_terms, term_left, term_right, shifts, block_sizes):
    blocks, nq, depth, _ = two_site.shape
    width = left_env.shape[0]
    nmpo = lax.axis_size("mpo")
    npl = nq // nmpo
    total = blocks * lax.axis_size("blk")
    first = lax.axis_index("blk") * blocks
    p_first = lax.axis_index("mpo") * npl

    local_terms = mpo_terms.shape[0]
    packed = jnp.concatenate(
        [mpo_terms.reshape(local_terms, nq * nq),
         term_left[:, None].astype(mpo_terms.dtype),
         term_right[:, None].astype(mpo_terms.dtype)], axis=1).astype(jnp.float32)
    packed = gather_terms(packed)
    nt = packed.shape[0]
    terms = packed[:, :nq * nq].reshape(nt, nq, nq).astype(mpo_terms.dtype)
    tl = packed[:, nq * nq].astype(jnp.int32)
    tr = packed[:, nq * nq + 1].astype(jnp.int32)

    ids = jnp.stack([first, p_first]).astype(jnp.int32)

    mine = lax.dynamic_slice_in_dim(terms, p_first, npl, axis=1).reshape(nt * npl, nq)
    mq = jnp.repeat(mine, YT, axis=1)

    lo, hi = halos(right_env, "blk", 1, SH)

    scalars = (tl, tr, block_sizes, shifts, ids)
    inner = block_call(*scalars, two_site, left_env, mq, right_env, None, None, None, npl=npl)
    return block_call(*scalars, two_site, left_env, mq, right_env, lo, hi, inner, npl=npl)


def block_call(tl, tr, block_sizes, shifts, ids, two_site, left_env, mq, right_env,
               lo, hi, prev, npl):
    blocks, nq, depth, _ = two_site.shape
    total = block_sizes.shape[0]
    halo = prev is not None
    if halo:
        base, stride, steps = 0, blocks - 1, 2
    else:
        base, stride, steps = 1, 1, blocks - 2
    width = left_env.shape[0]
    nt = tl.shape[0]
    rblock = (width, 1, depth, depth)

    def rloc_map(p):
        def index(b, tl_r, tr_r, bs_r, sh_r, ids_r):
            return (0, jnp.clip(base + b * stride + sh_r[ids_r[1] + p], 0, blocks - 1), 0, 0)
        return index

    const4 = lambda b, *refs: (0, 0, 0, 0)
    in_specs = [
        pl.BlockSpec((1, nq, depth, depth), lambda b, *refs: (base + b * stride, 0, 0, 0)),
        pl.BlockSpec(rblock, lambda b, *refs: (0, base + b * stride, 0, 0)),
        pl.BlockSpec(mq.shape, lambda b, *refs: (0, 0)),
        pl.BlockSpec(rblock, rloc_map(0)),
        pl.BlockSpec(rblock, rloc_map(1)),
    ]
    operands = [two_site, left_env, mq, right_env, right_env]
    aliases = {}
    if halo:
        in_specs += [pl.BlockSpec(rblock, const4), pl.BlockSpec(rblock, const4),
                     pl.BlockSpec(memory_space=pl.ANY)]
        operands += [lo, hi, prev]
        aliases = {5 + len(operands) - 1: 0}
    grid_spec = pltpu.PrefetchScalarGridSpec(
        num_scalar_prefetch=5,
        grid=(steps,),
        in_specs=in_specs,
        out_specs=pl.BlockSpec((1, npl, depth, depth),
                               lambda b, *refs: (base + b * stride, 0, 0, 0)),
        scratch_shapes=[
            pltpu.VMEM((nq, depth, depth), jnp.bfloat16),
            pltpu.VMEM((nt * npl, depth, depth), jnp.bfloat16),
            pltpu.VMEM((npl, nt, depth, depth), jnp.bfloat16),
            pltpu.VMEM((nt * npl * YT, nq * YT), jnp.bfloat16),
        ],
    )
    flops = 2 * steps * (nt * npl * YT * nq * YT * depth + 2 * nt * npl * depth ** 3)
    return pl.pallas_call(
        functools.partial(kernel, npl, nt, base, stride, blocks, total, halo),
        out_shape=jax.ShapeDtypeStruct((blocks, npl, depth, depth), jnp.bfloat16),
        grid_spec=grid_spec,
        compiler_params=pltpu.CompilerParams(
            dimension_semantics=("arbitrary",), vmem_limit_bytes=60 * 1024 * 1024),
        cost_estimate=pl.CostEstimate(
            flops=flops, transcendentals=0,
            bytes_accessed=2 * steps * (two_site.size + left_env.size + 3 * right_env.size)
            // blocks),
        input_output_aliases=aliases,
    )(tl, tr, block_sizes, shifts, ids, *operands)


def solution(mesh):
    return jax.shard_map(
        body,
        mesh=mesh,
        in_specs=(
            P("blk", None, None, None),
            P(None, "blk", None, None),
            P(None, "blk", None, None),
            P("mpo", None, None),
            P("mpo"),
            P("mpo"),
            P(),
            P(),
        ),
        out_specs=P("blk", "mpo", None, None),
        check_vma=False,
    )
```

```python
import functools

import jax
import jax.numpy as jnp
from jax import lax
from jax.experimental import pallas as pl
from jax.experimental.pallas import tpu as pltpu
from jax.sharding import PartitionSpec as P

SH = 1
YT = 16
UNROLL = 32
RUNROLL = 16
VARIANT = ""
RG = 4
RCHUNK = 64


def kernel(npl, nt, base, stride, nb, total, halo, *refs):
    (idx_ref, bs_ref, sh_ref, ids_ref,
     ts_ref, left_ref, mq_ref, rloc0_ref, rloc1_ref) = refs[:9]
    if halo:
        lo_ref, hi_ref = refs[9:11]
        refs = refs[12:]
    else:
        refs = refs[9:]
    per = idx_ref.shape[2]
    tl_of = lambda t: idx_ref[t // per, 0, t % per]
    tr_of = lambda t: idx_ref[t // per, 1, t % per]
    out_ref, c_scr, x_scr, y_scr, kron_scr = refs
    first_step = pl.program_id(0) == 0
    i = base + pl.program_id(0) * stride
    gi = ids_ref[0] + i

    def size_at(shift):
        j = gi + shift
        inside = (j >= 0) & (j < total)
        return jnp.where(inside, bs_ref[jnp.clip(j, 0, total - 1)], 0)

    sloc = [sh_ref[ids_ref[1] + p] for p in range(npl)]
    depth = ts_ref.shape[-1]
    nq = ts_ref.shape[1]
    rows = lax.broadcasted_iota(jnp.int32, (depth, depth), 0)
    cols = lax.broadcasted_iota(jnp.int32, (depth, depth), 1)
    row_ok = rows < bs_ref[gi]
    for q in range(nq):
        keep = row_ok & (cols < size_at(sh_ref[q]))
        c_scr[q] = jnp.where(keep, ts_ref[0, q], jnp.zeros_like(ts_ref[0, q]))

    nr = npl * nt
    rchunk = RCHUNK

    @pl.when(first_step)
    def _():
        a = lax.broadcasted_iota(jnp.int32, (nr * YT, nr), 0)
        r = lax.broadcasted_iota(jnp.int32, (nr * YT, nr), 1)
        pick = jnp.where(a // YT == r, 1.0, 0.0).astype(mq_ref.dtype)
        rep = jnp.dot(pick, mq_ref[...], preferred_element_type=jnp.float32)
        ra = lax.broadcasted_iota(jnp.int32, rep.shape, 0)
        cb = lax.broadcasted_iota(jnp.int32, rep.shape, 1)
        kron_scr[...] = jnp.where(ra % YT == cb % YT, rep, 0.0).astype(kron_scr.dtype)

    for yb in range(0 if "nomix" in VARIANT else depth // (2 * YT)):
        ya, yc = 2 * yb * YT, (2 * yb + 1) * YT
        cy = jnp.concatenate(
            [c_scr[:, ya:ya + YT, :].reshape(nq * YT, depth),
             c_scr[:, yc:yc + YT, :].reshape(nq * YT, depth)], axis=1)
        for rc in range(nr // rchunk):
            k = kron_scr[rc * rchunk * YT:(rc + 1) * rchunk * YT, :]
            xy = jnp.dot(k, cy, preferred_element_type=jnp.float32)
            for half, y0 in enumerate((ya, yc)):
                x_scr[rc * rchunk:(rc + 1) * rchunk, y0:y0 + YT, :] = (
                    xy[:, half * depth:(half + 1) * depth]
                    .reshape(rchunk, YT, depth).astype(x_scr.dtype))

    def left_step(t, carry):
        lt = left_ref[tl_of(t), 0]
        xs = jnp.concatenate([x_scr[t * npl + p] for p in range(npl)], axis=1)
        yt = jnp.dot(lt, xs, preferred_element_type=jnp.float32).astype(y_scr.dtype)
        for p in range(npl):
            y_scr[p, t] = yt[:, p * depth:(p + 1) * depth]
        return carry

    if "noleft" not in VARIANT:
        lax.fori_loop(0, nt, left_step, 0, unroll=UNROLL)

    def right_sum(p, src):
        def step(u, acc):
            ts_ = [RG * u + g for g in range(RG)]
            lhs = jnp.concatenate([y_scr[p, t] for t in ts_], axis=1)
            rhs = jnp.concatenate([src[tr_of(t), 0] for t in ts_], axis=0)
            return acc + jnp.dot(lhs, rhs, preferred_element_type=jnp.float32)
        acc = lax.fori_loop(0, nt // RG, step, jnp.zeros((depth, depth), jnp.float32),
                            unroll=RUNROLL)
        keep = row_ok & (cols < size_at(sloc[p]))
        out_ref[0, p] = jnp.where(keep, acc, 0.0).astype(out_ref.dtype)

    for p, rloc in enumerate(() if "noright" in VARIANT else (rloc0_ref, rloc1_ref)):
        if not halo:
            right_sum(p, rloc)
            continue
        j = i + sloc[p]

        @pl.when(j < 0)
        def _():
            right_sum(p, lo_ref)

        @pl.when((j >= 0) & (j < nb))
        def _():
            right_sum(p, rloc)

        @pl.when(j >= nb)
        def _():
            right_sum(p, hi_ref)


def gather_kernel(nm, x_ref, idx_ref, out_ref, idx_out_ref, send_sem, recv_sem,
                  isend_sem, irecv_sem):
    me = lax.axis_index("mpo")
    barrier = pltpu.get_barrier_semaphore()
    for d in range(1, nm):
        pl.semaphore_signal(barrier, inc=1, device_id={"mpo": lax.rem(me + d, nm)},
                            device_id_type=pl.DeviceIdType.MESH)
    pl.semaphore_wait(barrier, nm - 1)
    copies = []
    for d in range(1, nm):
        peer = lax.rem(me + d, nm)
        for src, dst, ssem, rsem in ((x_ref.at[peer], out_ref.at[me], send_sem, recv_sem),
                                     (idx_ref, idx_out_ref.at[me], isend_sem, irecv_sem)):
            copy = pltpu.make_async_remote_copy(
                src_ref=src,
                dst_ref=dst,
                send_sem=ssem.at[d],
                recv_sem=rsem.at[d],
                device_id={"mpo": peer},
                device_id_type=pl.DeviceIdType.MESH,
            )
            copy.start()
            copies.append(copy)
    out_ref[me] = x_ref[me]
    idx_out_ref[me] = idx_ref[...]
    for copy in copies:
        copy.wait()


def gather_terms(rows, idx):
    nm = lax.axis_size("mpo")
    sems = [pltpu.SemaphoreType.DMA((nm,)) for _ in range(4)]
    return pl.pallas_call(
        functools.partial(gather_kernel, nm),
        out_shape=(jax.ShapeDtypeStruct(rows.shape, rows.dtype),
                   jax.ShapeDtypeStruct((nm,) + idx.shape, idx.dtype)),
        in_specs=[pl.BlockSpec(memory_space=pltpu.VMEM)] * 2,
        out_specs=(pl.BlockSpec(memory_space=pltpu.VMEM),) * 2,
        scratch_shapes=sems,
        compiler_params=pltpu.CompilerParams(collective_id=0, has_side_effects=True),
    )(rows, idx)


def halos(cells, axis, dim, width):
    count = lax.axis_size(axis)
    ends = count - 1
    head = lax.slice_in_dim(cells, 0, width, axis=dim)
    tail = lax.slice_in_dim(cells, cells.shape[dim] - width, cells.shape[dim], axis=dim)
    lo = lax.ppermute(tail, axis, [(i, i + 1) for i in range(ends)])
    hi = lax.ppermute(head, axis, [(i + 1, i) for i in range(ends)])
    return lo, hi


def body(two_site, left_env, right_env, mpo_terms, term_left, term_right, shifts, block_sizes):
    blocks, nq, depth, _ = two_site.shape
    width = left_env.shape[0]
    nmpo = lax.axis_size("mpo")
    npl = nq // nmpo
    total = blocks * lax.axis_size("blk")
    first = lax.axis_index("blk") * blocks
    p_first = lax.axis_index("mpo") * npl

    local_terms = mpo_terms.shape[0]
    rows = mpo_terms.reshape(local_terms, nmpo, npl, nq).transpose(1, 0, 2, 3)
    rows = jnp.repeat(rows.reshape(nmpo, local_terms * npl, nq), YT, axis=2)
    idx = jnp.stack([term_left, term_right]).astype(jnp.int32)
    mq, idx = gather_terms(rows, idx)
    nt = nmpo * local_terms
    mq = mq.reshape(nt * npl, nq * YT)
    ids = jnp.stack([first, p_first]).astype(jnp.int32)

    lo, hi = halos(right_env, "blk", 1, SH)

    scalars = (idx, block_sizes, shifts, ids)
    inner = block_call(*scalars, two_site, left_env, mq, right_env, None, None, None, npl=npl)
    return block_call(*scalars, two_site, left_env, mq, right_env, lo, hi, inner, npl=npl)


def block_call(idx, block_sizes, shifts, ids, two_site, left_env, mq, right_env,
               lo, hi, prev, npl):
    blocks, nq, depth, _ = two_site.shape
    total = block_sizes.shape[0]
    halo = prev is not None
    if halo:
        base, stride, steps = 0, blocks - 1, 2
    else:
        base, stride, steps = 1, 1, blocks - 2
    width = left_env.shape[0]
    nt = idx.shape[0] * idx.shape[2]
    rblock = (width, 1, depth, depth)

    def rloc_map(p):
        def index(b, idx_r, bs_r, sh_r, ids_r):
            return (0, jnp.clip(base + b * stride + sh_r[ids_r[1] + p], 0, blocks - 1), 0, 0)
        return index

    const4 = lambda b, *refs: (0, 0, 0, 0)
    in_specs = [
        pl.BlockSpec((1, nq, depth, depth), lambda b, *refs: (base + b * stride, 0, 0, 0)),
        pl.BlockSpec(rblock, lambda b, *refs: (0, base + b * stride, 0, 0)),
        pl.BlockSpec(mq.shape, lambda b, *refs: (0, 0)),
        pl.BlockSpec(rblock, rloc_map(0)),
        pl.BlockSpec(rblock, rloc_map(1)),
    ]
    operands = [two_site, left_env, mq, right_env, right_env]
    aliases = {}
    if halo:
        in_specs += [pl.BlockSpec(rblock, const4), pl.BlockSpec(rblock, const4),
                     pl.BlockSpec(memory_space=pl.ANY)]
        operands += [lo, hi, prev]
        aliases = {4 + len(operands) - 1: 0}
    grid_spec = pltpu.PrefetchScalarGridSpec(
        num_scalar_prefetch=4,
        grid=(steps,),
        in_specs=in_specs,
        out_specs=pl.BlockSpec((1, npl, depth, depth),
                               lambda b, *refs: (base + b * stride, 0, 0, 0)),
        scratch_shapes=[
            pltpu.VMEM((nq, depth, depth), jnp.bfloat16),
            pltpu.VMEM((nt * npl, depth, depth), jnp.bfloat16),
            pltpu.VMEM((npl, nt, depth, depth), jnp.bfloat16),
            pltpu.VMEM((nt * npl * YT, nq * YT), jnp.bfloat16),
        ],
    )
    flops = 2 * steps * (nt * npl * YT * nq * YT * depth + 2 * nt * npl * depth ** 3)
    return pl.pallas_call(
        functools.partial(kernel, npl, nt, base, stride, blocks, total, halo),
        out_shape=jax.ShapeDtypeStruct((blocks, npl, depth, depth), jnp.bfloat16),
        grid_spec=grid_spec,
        compiler_params=pltpu.CompilerParams(
            dimension_semantics=("arbitrary",), vmem_limit_bytes=60 * 1024 * 1024),
        cost_estimate=pl.CostEstimate(
            flops=flops, transcendentals=0,
            bytes_accessed=2 * steps * (two_site.size + left_env.size + 3 * right_env.size)
            // blocks),
        input_output_aliases=aliases,
    )(idx, block_sizes, shifts, ids, *operands)


def solution(mesh):
    return jax.shard_map(
        body,
        mesh=mesh,
        in_specs=(
            P("blk", None, None, None),
            P(None, "blk", None, None),
            P(None, "blk", None, None),
            P("mpo", None, None),
            P("mpo"),
            P("mpo"),
            P(),
            P(),
        ),
        out_specs=P("blk", "mpo", None, None),
        check_vma=False,
    )
```

```python
import functools

import jax
import jax.numpy as jnp
from jax import lax
from jax.experimental import pallas as pl
from jax.experimental.pallas import tpu as pltpu
from jax.sharding import PartitionSpec as P

SH = 1
YT = 16
UNROLL = 32
RUNROLL = 16
VARIANT = ""
RG = 4
RCHUNK = 64


def kernel(npl, nt, base, stride, nb, total, halo, *refs):
    (idx_ref, bs_ref, sh_ref, ids_ref,
     ts_ref, left_ref, mq_ref, rloc0_ref, rloc1_ref) = refs[:9]
    if halo:
        lo_ref, hi_ref = refs[9:11]
        refs = refs[12:]
    else:
        refs = refs[9:]
    per = idx_ref.shape[2]
    tl_of = lambda t: idx_ref[t // per, 0, t % per]
    tr_of = lambda t: idx_ref[t // per, 1, t % per]
    out_ref, c_scr, x_scr, y_scr, kron_scr = refs
    first_step = pl.program_id(0) == 0
    i = base + pl.program_id(0) * stride
    gi = ids_ref[0] + i

    def size_at(shift):
        j = gi + shift
        inside = (j >= 0) & (j < total)
        return jnp.where(inside, bs_ref[jnp.clip(j, 0, total - 1)], 0)

    sloc = [sh_ref[ids_ref[1] + p] for p in range(npl)]
    depth = ts_ref.shape[-1]
    nq = ts_ref.shape[1]
    rows = lax.broadcasted_iota(jnp.int32, (depth, depth), 0)
    cols = lax.broadcasted_iota(jnp.int32, (depth, depth), 1)
    row_ok = rows < bs_ref[gi]
    for q in range(nq):
        keep = row_ok & (cols < size_at(sh_ref[q]))
        c_scr[q] = jnp.where(keep, ts_ref[0, q], jnp.zeros_like(ts_ref[0, q]))

    nr = npl * nt
    rchunk = RCHUNK

    @pl.when(first_step)
    def _():
        a = lax.broadcasted_iota(jnp.int32, (nr * YT, nr), 0)
        r = lax.broadcasted_iota(jnp.int32, (nr * YT, nr), 1)
        pick = jnp.where(a // YT == r, 1.0, 0.0).astype(mq_ref.dtype)
        rep = jnp.dot(pick, mq_ref[...], preferred_element_type=jnp.float32)
        ra = lax.broadcasted_iota(jnp.int32, rep.shape, 0)
        cb = lax.broadcasted_iota(jnp.int32, rep.shape, 1)
        kron_scr[...] = jnp.where(ra % YT == cb % YT, rep, 0.0).astype(kron_scr.dtype)

    for yb in range(0 if "nomix" in VARIANT else depth // (2 * YT)):
        ya, yc = 2 * yb * YT, (2 * yb + 1) * YT
        cy = jnp.concatenate(
            [c_scr[:, ya:ya + YT, :].reshape(nq * YT, depth),
             c_scr[:, yc:yc + YT, :].reshape(nq * YT, depth)], axis=1)
        for rc in range(nr // rchunk):
            k = kron_scr[rc * rchunk * YT:(rc + 1) * rchunk * YT, :]
            xy = jnp.dot(k, cy, preferred_element_type=jnp.float32)
            for half, y0 in enumerate((ya, yc)):
                x_scr[rc * rchunk:(rc + 1) * rchunk, y0:y0 + YT, :] = (
                    xy[:, half * depth:(half + 1) * depth]
                    .reshape(rchunk, YT, depth).astype(x_scr.dtype))

    def left_step(t, carry):
        lt = left_ref[tl_of(t), 0]
        xs = jnp.concatenate([x_scr[t * npl + p] for p in range(npl)], axis=1)
        yt = jnp.dot(lt, xs, preferred_element_type=jnp.float32).astype(y_scr.dtype)
        for p in range(npl):
            y_scr[p, t] = yt[:, p * depth:(p + 1) * depth]
        return carry

    if "noleft" not in VARIANT:
        lax.fori_loop(0, nt, left_step, 0, unroll=UNROLL)

    def right_sum(p, src):
        def step(u, acc):
            ts_ = [RG * u + g for g in range(RG)]
            lhs = jnp.concatenate([y_scr[p, t] for t in ts_], axis=1)
            rhs = jnp.concatenate([src[tr_of(t), 0] for t in ts_], axis=0)
            return acc + jnp.dot(lhs, rhs, preferred_element_type=jnp.float32)
        acc = lax.fori_loop(0, nt // RG, step, jnp.zeros((depth, depth), jnp.float32),
                            unroll=RUNROLL)
        keep = row_ok & (cols < size_at(sloc[p]))
        out_ref[0, p] = jnp.where(keep, acc, 0.0).astype(out_ref.dtype)

    for p, rloc in enumerate(() if "noright" in VARIANT else (rloc0_ref, rloc1_ref)):
        if not halo:
            right_sum(p, rloc)
            continue
        j = i + sloc[p]

        @pl.when(j < 0)
        def _():
            right_sum(p, lo_ref)

        @pl.when((j >= 0) & (j < nb))
        def _():
            right_sum(p, rloc)

        @pl.when(j >= nb)
        def _():
            right_sum(p, hi_ref)


def gather_kernel(nm, x_ref, idx_ref, out_ref, idx_out_ref, send_sem, recv_sem,
                  isend_sem, irecv_sem):
    me = lax.axis_index("mpo")
    barrier = pltpu.get_barrier_semaphore()
    for d in range(1, nm):
        pl.semaphore_signal(barrier, inc=1, device_id={"mpo": lax.rem(me + d, nm)},
                            device_id_type=pl.DeviceIdType.MESH)
    pl.semaphore_wait(barrier, nm - 1)
    copies = []
    for d in range(1, nm):
        peer = lax.rem(me + d, nm)
        for src, dst, ssem, rsem in ((x_ref.at[peer], out_ref.at[me], send_sem, recv_sem),
                                     (idx_ref, idx_out_ref.at[me], isend_sem, irecv_sem)):
            copy = pltpu.make_async_remote_copy(
                src_ref=src,
                dst_ref=dst,
                send_sem=ssem.at[d],
                recv_sem=rsem.at[d],
                device_id={"mpo": peer},
                device_id_type=pl.DeviceIdType.MESH,
            )
            copy.start()
            copies.append(copy)
    out_ref[me] = x_ref[me]
    idx_out_ref[me] = idx_ref[...]
    for copy in copies:
        copy.wait()


def gather_terms(rows, idx):
    nm = lax.axis_size("mpo")
    sems = [pltpu.SemaphoreType.DMA((nm,)) for _ in range(4)]
    return pl.pallas_call(
        functools.partial(gather_kernel, nm),
        out_shape=(jax.ShapeDtypeStruct(rows.shape, rows.dtype),
                   jax.ShapeDtypeStruct((nm,) + idx.shape, idx.dtype)),
        in_specs=[pl.BlockSpec(memory_space=pltpu.VMEM)] * 2,
        out_specs=(pl.BlockSpec(memory_space=pltpu.VMEM),) * 2,
        scratch_shapes=sems,
        compiler_params=pltpu.CompilerParams(collective_id=0, has_side_effects=True),
    )(rows, idx)


def halos(cells, axis, dim, width):
    count = lax.axis_size(axis)
    ends = count - 1
    head = lax.slice_in_dim(cells, 0, width, axis=dim)
    tail = lax.slice_in_dim(cells, cells.shape[dim] - width, cells.shape[dim], axis=dim)
    lo = lax.ppermute(tail, axis, [(i, i + 1) for i in range(ends)])
    hi = lax.ppermute(head, axis, [(i + 1, i) for i in range(ends)])
    return lo, hi


def body(two_site, left_env, right_env, mpo_terms, term_left, term_right, shifts, block_sizes):
    blocks, nq, depth, _ = two_site.shape
    width = left_env.shape[0]
    nmpo = lax.axis_size("mpo")
    npl = nq // nmpo
    total = blocks * lax.axis_size("blk")
    first = lax.axis_index("blk") * blocks
    p_first = lax.axis_index("mpo") * npl

    local_terms = mpo_terms.shape[0]
    rows = mpo_terms.reshape(local_terms, nmpo, npl, nq).transpose(1, 0, 2, 3)
    rows = jnp.repeat(rows.reshape(nmpo, local_terms * npl, nq), YT, axis=2)
    idx = jnp.stack([term_left, term_right]).astype(jnp.int32)
    mq, idx = gather_terms(rows, idx)
    nt = nmpo * local_terms
    mq = mq.reshape(nt * npl, nq * YT)
    ids = jnp.stack([first, p_first]).astype(jnp.int32)

    lo, hi = halos(right_env, "blk", 1, SH)

    scalars = (idx, block_sizes, shifts, ids)
    inner = block_call(*scalars, two_site, left_env, mq, right_env, None, None, None, npl=npl)
    return block_call(*scalars, two_site, left_env, mq, right_env, lo, hi, inner, npl=npl)


def block_call(idx, block_sizes, shifts, ids, two_site, left_env, mq, right_env,
               lo, hi, prev, npl):
    blocks, nq, depth, _ = two_site.shape
    total = block_sizes.shape[0]
    halo = prev is not None
    if halo:
        base, stride, steps = 0, blocks - 1, 2
    else:
        base, stride, steps = 1, 1, blocks - 2
    width = left_env.shape[0]
    nt = idx.shape[0] * idx.shape[2]
    rblock = (width, 1, depth, depth)

    def rloc_map(p):
        def index(b, idx_r, bs_r, sh_r, ids_r):
            return (0, jnp.clip(base + b * stride + sh_r[ids_r[1] + p], 0, blocks - 1), 0, 0)
        return index

    const4 = lambda b, *refs: (0, 0, 0, 0)
    in_specs = [
        pl.BlockSpec((1, nq, depth, depth), lambda b, *refs: (base + b * stride, 0, 0, 0)),
        pl.BlockSpec(rblock, lambda b, *refs: (0, base + b * stride, 0, 0)),
        pl.BlockSpec(mq.shape, lambda b, *refs: (0, 0)),
        pl.BlockSpec(rblock, rloc_map(0)),
        pl.BlockSpec(rblock, rloc_map(1)),
    ]
    operands = [two_site, left_env, mq, right_env, right_env]
    aliases = {}
    if halo:
        in_specs += [pl.BlockSpec(memory_space=pltpu.VMEM), pl.BlockSpec(memory_space=pltpu.VMEM),
                     pl.BlockSpec(memory_space=pl.ANY)]
        operands += [lo, hi, prev]
        aliases = {4 + len(operands) - 1: 0}
    grid_spec = pltpu.PrefetchScalarGridSpec(
        num_scalar_prefetch=4,
        grid=(steps,),
        in_specs=in_specs,
        out_specs=pl.BlockSpec((1, npl, depth, depth),
                               lambda b, *refs: (base + b * stride, 0, 0, 0)),
        scratch_shapes=[
            pltpu.VMEM((nq, depth, depth), jnp.bfloat16),
            pltpu.VMEM((nt * npl, depth, depth), jnp.bfloat16),
            pltpu.VMEM((npl, nt, depth, depth), jnp.bfloat16),
            pltpu.VMEM((nt * npl * YT, nq * YT), jnp.bfloat16),
        ],
    )
    flops = 2 * steps * (nt * npl * YT * nq * YT * depth + 2 * nt * npl * depth ** 3)
    return pl.pallas_call(
        functools.partial(kernel, npl, nt, base, stride, blocks, total, halo),
        out_shape=jax.ShapeDtypeStruct((blocks, npl, depth, depth), jnp.bfloat16),
        grid_spec=grid_spec,
        compiler_params=pltpu.CompilerParams(
            dimension_semantics=("arbitrary",), vmem_limit_bytes=(48 if halo else 60) * 1024 * 1024),
        cost_estimate=pl.CostEstimate(
            flops=flops, transcendentals=0,
            bytes_accessed=2 * steps * (two_site.size + left_env.size + 3 * right_env.size)
            // blocks),
        input_output_aliases=aliases,
    )(idx, block_sizes, shifts, ids, *operands)


def solution(mesh):
    return jax.shard_map(
        body,
        mesh=mesh,
        in_specs=(
            P("blk", None, None, None),
            P(None, "blk", None, None),
            P(None, "blk", None, None),
            P("mpo", None, None),
            P("mpo"),
            P("mpo"),
            P(),
            P(),
        ),
        out_specs=P("blk", "mpo", None, None),
        check_vma=False,
    )
```

```python
import functools

import jax
import jax.numpy as jnp
from jax import lax
from jax.experimental import pallas as pl
from jax.experimental.pallas import tpu as pltpu
from jax.sharding import PartitionSpec as P

SH = 1
YT = 16
UNROLL = 32
RUNROLL = 16
VARIANT = ""
RG = 4
RCHUNK = 64


def kernel(npl, nt, base, stride, nb, total, halo, *refs):
    (idx_ref, bs_ref, sh_ref, ids_ref,
     ts_ref, left_ref, mq_ref, rloc0_ref, rloc1_ref) = refs[:9]
    if halo:
        lo_ref, hi_ref, kron_scr = refs[9:12]
        out_ref, c_scr, x_scr, y_scr = refs[13:]
    else:
        out_ref, kron_scr, c_scr, x_scr, y_scr = refs[9:]
    per = idx_ref.shape[2]
    tl_of = lambda t: idx_ref[t // per, 0, t % per]
    tr_of = lambda t: idx_ref[t // per, 1, t % per]
    first_step = pl.program_id(0) == 0
    i = base + pl.program_id(0) * stride
    gi = ids_ref[0] + i

    def size_at(shift):
        j = gi + shift
        inside = (j >= 0) & (j < total)
        return jnp.where(inside, bs_ref[jnp.clip(j, 0, total - 1)], 0)

    sloc = [sh_ref[ids_ref[1] + p] for p in range(npl)]
    depth = ts_ref.shape[-1]
    nq = ts_ref.shape[1]
    rows = lax.broadcasted_iota(jnp.int32, (depth, depth), 0)
    cols = lax.broadcasted_iota(jnp.int32, (depth, depth), 1)
    row_ok = rows < bs_ref[gi]
    for q in range(nq):
        keep = row_ok & (cols < size_at(sh_ref[q]))
        c_scr[q] = jnp.where(keep, ts_ref[0, q], jnp.zeros_like(ts_ref[0, q]))

    nr = npl * nt
    rchunk = RCHUNK

    if not halo:
        @pl.when(first_step)
        def _():
            a = lax.broadcasted_iota(jnp.int32, (nr * YT, nr), 0)
            r = lax.broadcasted_iota(jnp.int32, (nr * YT, nr), 1)
            pick = jnp.where(a // YT == r, 1.0, 0.0).astype(mq_ref.dtype)
            rep = jnp.dot(pick, mq_ref[...], preferred_element_type=jnp.float32)
            ra = lax.broadcasted_iota(jnp.int32, rep.shape, 0)
            cb = lax.broadcasted_iota(jnp.int32, rep.shape, 1)
            kron_scr[...] = jnp.where(ra % YT == cb % YT, rep, 0.0).astype(kron_scr.dtype)

    for yb in range(0 if "nomix" in VARIANT else depth // (2 * YT)):
        ya, yc = 2 * yb * YT, (2 * yb + 1) * YT
        cy = jnp.concatenate(
            [c_scr[:, ya:ya + YT, :].reshape(nq * YT, depth),
             c_scr[:, yc:yc + YT, :].reshape(nq * YT, depth)], axis=1)
        for rc in range(nr // rchunk):
            k = kron_scr[rc * rchunk * YT:(rc + 1) * rchunk * YT, :]
            xy = jnp.dot(k, cy, preferred_element_type=jnp.float32)
            for half, y0 in enumerate((ya, yc)):
                x_scr[rc * rchunk:(rc + 1) * rchunk, y0:y0 + YT, :] = (
                    xy[:, half * depth:(half + 1) * depth]
                    .reshape(rchunk, YT, depth).astype(x_scr.dtype))

    def left_step(t, carry):
        lt = left_ref[tl_of(t), 0]
        xs = jnp.concatenate([x_scr[t * npl + p] for p in range(npl)], axis=1)
        yt = jnp.dot(lt, xs, preferred_element_type=jnp.float32).astype(y_scr.dtype)
        for p in range(npl):
            y_scr[p, t] = yt[:, p * depth:(p + 1) * depth]
        return carry

    if "noleft" not in VARIANT:
        lax.fori_loop(0, nt, left_step, 0, unroll=UNROLL)

    def right_sum(p, src):
        def step(u, acc):
            ts_ = [RG * u + g for g in range(RG)]
            lhs = jnp.concatenate([y_scr[p, t] for t in ts_], axis=1)
            rhs = jnp.concatenate([src[tr_of(t), 0] for t in ts_], axis=0)
            return acc + jnp.dot(lhs, rhs, preferred_element_type=jnp.float32)
        acc = lax.fori_loop(0, nt // RG, step, jnp.zeros((depth, depth), jnp.float32),
                            unroll=RUNROLL)
        keep = row_ok & (cols < size_at(sloc[p]))
        out_ref[0, p] = jnp.where(keep, acc, 0.0).astype(out_ref.dtype)

    for p, rloc in enumerate(() if "noright" in VARIANT else (rloc0_ref, rloc1_ref)):
        if not halo:
            right_sum(p, rloc)
            continue
        j = i + sloc[p]

        @pl.when(j < 0)
        def _():
            right_sum(p, lo_ref)

        @pl.when((j >= 0) & (j < nb))
        def _():
            right_sum(p, rloc)

        @pl.when(j >= nb)
        def _():
            right_sum(p, hi_ref)


def gather_kernel(nm, x_ref, idx_ref, out_ref, idx_out_ref, send_sem, recv_sem,
                  isend_sem, irecv_sem):
    me = lax.axis_index("mpo")
    barrier = pltpu.get_barrier_semaphore()
    for d in range(1, nm):
        pl.semaphore_signal(barrier, inc=1, device_id={"mpo": lax.rem(me + d, nm)},
                            device_id_type=pl.DeviceIdType.MESH)
    pl.semaphore_wait(barrier, nm - 1)
    copies = []
    for d in range(1, nm):
        peer = lax.rem(me + d, nm)
        for src, dst, ssem, rsem in ((x_ref.at[peer], out_ref.at[me], send_sem, recv_sem),
                                     (idx_ref, idx_out_ref.at[me], isend_sem, irecv_sem)):
            copy = pltpu.make_async_remote_copy(
                src_ref=src,
                dst_ref=dst,
                send_sem=ssem.at[d],
                recv_sem=rsem.at[d],
                device_id={"mpo": peer},
                device_id_type=pl.DeviceIdType.MESH,
            )
            copy.start()
            copies.append(copy)
    out_ref[me] = x_ref[me]
    idx_out_ref[me] = idx_ref[...]
    for copy in copies:
        copy.wait()


def gather_terms(rows, idx):
    nm = lax.axis_size("mpo")
    sems = [pltpu.SemaphoreType.DMA((nm,)) for _ in range(4)]
    return pl.pallas_call(
        functools.partial(gather_kernel, nm),
        out_shape=(jax.ShapeDtypeStruct(rows.shape, rows.dtype),
                   jax.ShapeDtypeStruct((nm,) + idx.shape, idx.dtype)),
        in_specs=[pl.BlockSpec(memory_space=pltpu.VMEM)] * 2,
        out_specs=(pl.BlockSpec(memory_space=pltpu.VMEM),) * 2,
        scratch_shapes=sems,
        compiler_params=pltpu.CompilerParams(collective_id=0, has_side_effects=True),
    )(rows, idx)


def halos(cells, axis, dim, width):
    count = lax.axis_size(axis)
    ends = count - 1
    head = lax.slice_in_dim(cells, 0, width, axis=dim)
    tail = lax.slice_in_dim(cells, cells.shape[dim] - width, cells.shape[dim], axis=dim)
    lo = lax.ppermute(tail, axis, [(i, i + 1) for i in range(ends)])
    hi = lax.ppermute(head, axis, [(i + 1, i) for i in range(ends)])
    return lo, hi


def body(two_site, left_env, right_env, mpo_terms, term_left, term_right, shifts, block_sizes):
    blocks, nq, depth, _ = two_site.shape
    width = left_env.shape[0]
    nmpo = lax.axis_size("mpo")
    npl = nq // nmpo
    total = blocks * lax.axis_size("blk")
    first = lax.axis_index("blk") * blocks
    p_first = lax.axis_index("mpo") * npl

    local_terms = mpo_terms.shape[0]
    rows = mpo_terms.reshape(local_terms, nmpo, npl, nq).transpose(1, 0, 2, 3)
    rows = jnp.repeat(rows.reshape(nmpo, local_terms * npl, nq), YT, axis=2)
    idx = jnp.stack([term_left, term_right]).astype(jnp.int32)
    mq, idx = gather_terms(rows, idx)
    nt = nmpo * local_terms
    mq = mq.reshape(nt * npl, nq * YT)
    ids = jnp.stack([first, p_first]).astype(jnp.int32)

    lo, hi = halos(right_env, "blk", 1, SH)

    scalars = (idx, block_sizes, shifts, ids)
    inner = block_call(*scalars, two_site, left_env, mq, right_env, None, None, None, npl=npl)
    inner, kron = inner
    return block_call(*scalars, two_site, left_env, kron, right_env, lo, hi, inner, npl=npl)


def block_call(idx, block_sizes, shifts, ids, two_site, left_env, mq, right_env,
               lo, hi, prev, npl):
    blocks, nq, depth, _ = two_site.shape
    total = block_sizes.shape[0]
    halo = prev is not None
    if halo:
        base, stride, steps = 0, blocks - 1, 2
    else:
        base, stride, steps = 1, 1, blocks - 2
    width = left_env.shape[0]
    nt = idx.shape[0] * idx.shape[2]
    rblock = (width, 1, depth, depth)

    def rloc_map(p):
        def index(b, idx_r, bs_r, sh_r, ids_r):
            return (0, jnp.clip(base + b * stride + sh_r[ids_r[1] + p], 0, blocks - 1), 0, 0)
        return index

    const4 = lambda b, *refs: (0, 0, 0, 0)
    in_specs = [
        pl.BlockSpec((1, nq, depth, depth), lambda b, *refs: (base + b * stride, 0, 0, 0)),
        pl.BlockSpec(rblock, lambda b, *refs: (0, base + b * stride, 0, 0)),
        pl.BlockSpec(mq.shape, lambda b, *refs: (0, 0)),
        pl.BlockSpec(rblock, rloc_map(0)),
        pl.BlockSpec(rblock, rloc_map(1)),
    ]
    operands = [two_site, left_env, mq, right_env, right_env]
    aliases = {}
    kron_shape = (nt * npl * YT, nq * YT)
    if halo:
        in_specs += [pl.BlockSpec(memory_space=pltpu.VMEM), pl.BlockSpec(memory_space=pltpu.VMEM),
                     pl.BlockSpec(kron_shape, lambda b, *refs: (0, 0)),
                     pl.BlockSpec(memory_space=pl.ANY)]
        operands += [lo, hi, mq, prev]
        aliases = {4 + len(operands) - 1: 0}
    out_block = pl.BlockSpec((1, npl, depth, depth), lambda b, *refs: (base + b * stride, 0, 0, 0))
    out_shape = jax.ShapeDtypeStruct((blocks, npl, depth, depth), jnp.bfloat16)
    if halo:
        out_specs = out_block
    else:
        out_specs = (out_block, pl.BlockSpec(kron_shape, lambda b, *refs: (0, 0)))
        out_shape = (out_shape, jax.ShapeDtypeStruct(kron_shape, jnp.bfloat16))
    grid_spec = pltpu.PrefetchScalarGridSpec(
        num_scalar_prefetch=4,
        grid=(steps,),
        in_specs=in_specs,
        out_specs=out_specs,
        scratch_shapes=[
            pltpu.VMEM((nq, depth, depth), jnp.bfloat16),
            pltpu.VMEM((nt * npl, depth, depth), jnp.bfloat16),
            pltpu.VMEM((npl, nt, depth, depth), jnp.bfloat16),
        ],
    )
    flops = 2 * steps * (nt * npl * YT * nq * YT * depth + 2 * nt * npl * depth ** 3)
    return pl.pallas_call(
        functools.partial(kernel, npl, nt, base, stride, blocks, total, halo),
        out_shape=out_shape,
        grid_spec=grid_spec,
        compiler_params=pltpu.CompilerParams(
            dimension_semantics=("arbitrary",), vmem_limit_bytes=(48 if halo else 60) * 1024 * 1024),
        cost_estimate=pl.CostEstimate(
            flops=flops, transcendentals=0,
            bytes_accessed=2 * steps * (two_site.size + left_env.size + 3 * right_env.size)
            // blocks),
        input_output_aliases=aliases,
    )(idx, block_sizes, shifts, ids, *operands)


def solution(mesh):
    return jax.shard_map(
        body,
        mesh=mesh,
        in_specs=(
            P("blk", None, None, None),
            P(None, "blk", None, None),
            P(None, "blk", None, None),
            P("mpo", None, None),
            P("mpo"),
            P("mpo"),
            P(),
            P(),
        ),
        out_specs=P("blk", "mpo", None, None),
        check_vma=False,
    )
```

```python
import functools

import jax
import jax.numpy as jnp
from jax import lax
from jax.experimental import pallas as pl
from jax.experimental.pallas import tpu as pltpu
from jax.sharding import PartitionSpec as P

SH = 1
YT = 16
UNROLL = 32
RUNROLL = 16
VARIANT = ""
RG = 4
RCHUNK = 64


def kernel(npl, nt, base, stride, nb, total, halo, *refs):
    (idx_ref, bs_ref, sh_ref, ids_ref,
     ts_ref, left_ref, mq_ref, rloc0_ref, rloc1_ref) = refs[:9]
    if halo:
        lo_ref, hi_ref = refs[9:11]
        refs = refs[12:]
    else:
        refs = refs[9:]
    per = idx_ref.shape[2]
    tl_of = lambda t: idx_ref[t // per, 0, t % per]
    tr_of = lambda t: idx_ref[t // per, 1, t % per]
    out_ref, c_scr, x_scr, y_scr, kron_scr = refs
    first_step = pl.program_id(0) == 0
    i = base + pl.program_id(0) * stride
    gi = ids_ref[0] + i

    def size_at(shift):
        j = gi + shift
        inside = (j >= 0) & (j < total)
        return jnp.where(inside, bs_ref[jnp.clip(j, 0, total - 1)], 0)

    sloc = [sh_ref[ids_ref[1] + p] for p in range(npl)]
    depth = ts_ref.shape[-1]
    nq = ts_ref.shape[1]
    rows = lax.broadcasted_iota(jnp.int32, (depth, depth), 0)
    cols = lax.broadcasted_iota(jnp.int32, (depth, depth), 1)
    row_ok = rows < bs_ref[gi]
    for q in range(nq):
        keep = row_ok & (cols < size_at(sh_ref[q]))
        c_scr[q] = jnp.where(keep, ts_ref[0, q], jnp.zeros_like(ts_ref[0, q]))

    nr = npl * nt
    rchunk = RCHUNK

    @pl.when(first_step)
    def _():
        a = lax.broadcasted_iota(jnp.int32, (nr * YT, nr), 0)
        r = lax.broadcasted_iota(jnp.int32, (nr * YT, nr), 1)
        pick = jnp.where(a // YT == r, 1.0, 0.0).astype(mq_ref.dtype)
        rep = jnp.dot(pick, mq_ref[...], preferred_element_type=jnp.float32)
        ra = lax.broadcasted_iota(jnp.int32, rep.shape, 0)
        cb = lax.broadcasted_iota(jnp.int32, rep.shape, 1)
        kron_scr[...] = jnp.where(ra % YT == cb % YT, rep, 0.0).astype(kron_scr.dtype)

    for yb in range(0 if "nomix" in VARIANT else depth // (2 * YT)):
        ya, yc = 2 * yb * YT, (2 * yb + 1) * YT
        cy = jnp.concatenate(
            [c_scr[:, ya:ya + YT, :].reshape(nq * YT, depth),
             c_scr[:, yc:yc + YT, :].reshape(nq * YT, depth)], axis=1)
        for rc in range(nr // rchunk):
            k = kron_scr[rc * rchunk * YT:(rc + 1) * rchunk * YT, :]
            xy = jnp.dot(k, cy, preferred_element_type=jnp.float32)
            for half, y0 in enumerate((ya, yc)):
                x_scr[rc * rchunk:(rc + 1) * rchunk, y0:y0 + YT, :] = (
                    xy[:, half * depth:(half + 1) * depth]
                    .reshape(rchunk, YT, depth).astype(x_scr.dtype))

    def left_step(t, carry):
        lt = left_ref[tl_of(t), 0]
        xs = jnp.concatenate([x_scr[t * npl + p] for p in range(npl)], axis=1)
        yt = jnp.dot(lt, xs, preferred_element_type=jnp.float32).astype(y_scr.dtype)
        for p in range(npl):
            y_scr[p, t] = yt[:, p * depth:(p + 1) * depth]
        return carry

    if "noleft" not in VARIANT:
        lax.fori_loop(0, nt, left_step, 0, unroll=UNROLL)

    def right_sum(p, src):
        def step(u, acc):
            ts_ = [RG * u + g for g in range(RG)]
            lhs = jnp.concatenate([y_scr[p, t] for t in ts_], axis=1)
            rhs = jnp.concatenate([src[tr_of(t), 0] for t in ts_], axis=0)
            return acc + jnp.dot(lhs, rhs, preferred_element_type=jnp.float32)
        acc = lax.fori_loop(0, nt // RG, step, jnp.zeros((depth, depth), jnp.float32),
                            unroll=RUNROLL)
        keep = row_ok & (cols < size_at(sloc[p]))
        out_ref[0, p] = jnp.where(keep, acc, 0.0).astype(out_ref.dtype)

    for p, rloc in enumerate(() if "noright" in VARIANT else (rloc0_ref, rloc1_ref)):
        if not halo:
            right_sum(p, rloc)
            continue
        j = i + sloc[p]

        @pl.when(j < 0)
        def _():
            right_sum(p, lo_ref)

        @pl.when((j >= 0) & (j < nb))
        def _():
            right_sum(p, rloc)

        @pl.when(j >= nb)
        def _():
            right_sum(p, hi_ref)


def gather_kernel(nm, x_ref, idx_ref, out_ref, idx_out_ref, send_sem, recv_sem,
                  isend_sem, irecv_sem):
    me = lax.axis_index("mpo")
    barrier = pltpu.get_barrier_semaphore()
    for d in range(1, nm):
        pl.semaphore_signal(barrier, inc=1, device_id={"mpo": lax.rem(me + d, nm)},
                            device_id_type=pl.DeviceIdType.MESH)
    pl.semaphore_wait(barrier, nm - 1)
    copies = []
    for d in range(1, nm):
        peer = lax.rem(me + d, nm)
        for src, dst, ssem, rsem in ((x_ref.at[peer], out_ref.at[me], send_sem, recv_sem),
                                     (idx_ref, idx_out_ref.at[me], isend_sem, irecv_sem)):
            copy = pltpu.make_async_remote_copy(
                src_ref=src,
                dst_ref=dst,
                send_sem=ssem.at[d],
                recv_sem=rsem.at[d],
                device_id={"mpo": peer},
                device_id_type=pl.DeviceIdType.MESH,
            )
            copy.start()
            copies.append(copy)
    out_ref[me] = x_ref[me]
    idx_out_ref[me] = idx_ref[...]
    for copy in copies:
        copy.wait()


def gather_terms(rows, idx):
    nm = lax.axis_size("mpo")
    sems = [pltpu.SemaphoreType.DMA((nm,)) for _ in range(4)]
    return pl.pallas_call(
        functools.partial(gather_kernel, nm),
        out_shape=(jax.ShapeDtypeStruct(rows.shape, rows.dtype),
                   jax.ShapeDtypeStruct((nm,) + idx.shape, idx.dtype)),
        in_specs=[pl.BlockSpec(memory_space=pltpu.VMEM)] * 2,
        out_specs=(pl.BlockSpec(memory_space=pltpu.VMEM),) * 2,
        scratch_shapes=sems,
        compiler_params=pltpu.CompilerParams(collective_id=0, has_side_effects=True),
    )(rows, idx)


def edge_kernel(width, src_ref, head_ref, tail_ref, sem):
    last = src_ref.shape[1] - width
    copies = [pltpu.make_async_copy(src_ref.at[:, pl.ds(0, width)], head_ref, sem.at[0]),
              pltpu.make_async_copy(src_ref.at[:, pl.ds(last, width)], tail_ref, sem.at[1])]
    for copy in copies:
        copy.start()
    for copy in copies:
        copy.wait()


def edges(cells, width):
    shape = (cells.shape[0], width) + cells.shape[2:]
    part = jax.ShapeDtypeStruct(shape, cells.dtype)
    return pl.pallas_call(
        functools.partial(edge_kernel, width),
        out_shape=(part, part),
        in_specs=[pl.BlockSpec(memory_space=pl.ANY)],
        out_specs=(pl.BlockSpec(memory_space=pltpu.VMEM),) * 2,
        scratch_shapes=[pltpu.SemaphoreType.DMA((2,))],
    )(cells)


def halos(cells, axis, dim, width):
    count = lax.axis_size(axis)
    ends = count - 1
    head, tail = edges(cells, width)
    lo = lax.ppermute(tail, axis, [(i, i + 1) for i in range(ends)])
    hi = lax.ppermute(head, axis, [(i + 1, i) for i in range(ends)])
    return lo, hi


def body(two_site, left_env, right_env, mpo_terms, term_left, term_right, shifts, block_sizes):
    blocks, nq, depth, _ = two_site.shape
    width = left_env.shape[0]
    nmpo = lax.axis_size("mpo")
    npl = nq // nmpo
    total = blocks * lax.axis_size("blk")
    first = lax.axis_index("blk") * blocks
    p_first = lax.axis_index("mpo") * npl

    local_terms = mpo_terms.shape[0]
    rows = mpo_terms.reshape(local_terms, nmpo, npl, nq).transpose(1, 0, 2, 3)
    rows = jnp.repeat(rows.reshape(nmpo, local_terms * npl, nq), YT, axis=2)
    idx = jnp.stack([term_left, term_right]).astype(jnp.int32)
    mq, idx = gather_terms(rows, idx)
    nt = nmpo * local_terms
    mq = mq.reshape(nt * npl, nq * YT)
    ids = jnp.stack([first, p_first]).astype(jnp.int32)

    lo, hi = halos(right_env, "blk", 1, SH)

    scalars = (idx, block_sizes, shifts, ids)
    inner = block_call(*scalars, two_site, left_env, mq, right_env, None, None, None, npl=npl)
    return block_call(*scalars, two_site, left_env, mq, right_env, lo, hi, inner, npl=npl)


def block_call(idx, block_sizes, shifts, ids, two_site, left_env, mq, right_env,
               lo, hi, prev, npl):
    blocks, nq, depth, _ = two_site.shape
    total = block_sizes.shape[0]
    halo = prev is not None
    if halo:
        base, stride, steps = 0, blocks - 1, 2
    else:
        base, stride, steps = 1, 1, blocks - 2
    width = left_env.shape[0]
    nt = idx.shape[0] * idx.shape[2]
    rblock = (width, 1, depth, depth)

    def rloc_map(p):
        def index(b, idx_r, bs_r, sh_r, ids_r):
            return (0, jnp.clip(base + b * stride + sh_r[ids_r[1] + p], 0, blocks - 1), 0, 0)
        return index

    const4 = lambda b, *refs: (0, 0, 0, 0)
    in_specs = [
        pl.BlockSpec((1, nq, depth, depth), lambda b, *refs: (base + b * stride, 0, 0, 0)),
        pl.BlockSpec(rblock, lambda b, *refs: (0, base + b * stride, 0, 0)),
        pl.BlockSpec(mq.shape, lambda b, *refs: (0, 0)),
        pl.BlockSpec(rblock, rloc_map(0)),
        pl.BlockSpec(rblock, rloc_map(1)),
    ]
    operands = [two_site, left_env, mq, right_env, right_env]
    aliases = {}
    if halo:
        in_specs += [pl.BlockSpec(memory_space=pltpu.VMEM), pl.BlockSpec(memory_space=pltpu.VMEM),
                     pl.BlockSpec(memory_space=pl.ANY)]
        operands += [lo, hi, prev]
        aliases = {4 + len(operands) - 1: 0}
    grid_spec = pltpu.PrefetchScalarGridSpec(
        num_scalar_prefetch=4,
        grid=(steps,),
        in_specs=in_specs,
        out_specs=pl.BlockSpec((1, npl, depth, depth),
                               lambda b, *refs: (base + b * stride, 0, 0, 0)),
        scratch_shapes=[
            pltpu.VMEM((nq, depth, depth), jnp.bfloat16),
            pltpu.VMEM((nt * npl, depth, depth), jnp.bfloat16),
            pltpu.VMEM((npl, nt, depth, depth), jnp.bfloat16),
            pltpu.VMEM((nt * npl * YT, nq * YT), jnp.bfloat16),
        ],
    )
    flops = 2 * steps * (nt * npl * YT * nq * YT * depth + 2 * nt * npl * depth ** 3)
    return pl.pallas_call(
        functools.partial(kernel, npl, nt, base, stride, blocks, total, halo),
        out_shape=jax.ShapeDtypeStruct((blocks, npl, depth, depth), jnp.bfloat16),
        grid_spec=grid_spec,
        compiler_params=pltpu.CompilerParams(
            dimension_semantics=("arbitrary",), vmem_limit_bytes=(48 if halo else 60) * 1024 * 1024),
        cost_estimate=pl.CostEstimate(
            flops=flops, transcendentals=0,
            bytes_accessed=2 * steps * (two_site.size + left_env.size + 3 * right_env.size)
            // blocks),
        input_output_aliases=aliases,
    )(idx, block_sizes, shifts, ids, *operands)


def solution(mesh):
    return jax.shard_map(
        body,
        mesh=mesh,
        in_specs=(
            P("blk", None, None, None),
            P(None, "blk", None, None),
            P(None, "blk", None, None),
            P("mpo", None, None),
            P("mpo"),
            P("mpo"),
            P(),
            P(),
        ),
        out_specs=P("blk", "mpo", None, None),
        check_vma=False,
    )
```

```python
import functools

import jax
import jax.numpy as jnp
from jax import lax
from jax.experimental import pallas as pl
from jax.experimental.pallas import tpu as pltpu
from jax.sharding import PartitionSpec as P

SH = 1
YT = 16
UNROLL = 32
RUNROLL = 16
VARIANT = ""
RG = 4
RCHUNK = 64


def kernel(npl, nt, base, stride, nb, total, halo, *refs):
    (idx_ref, bs_ref, sh_ref, ids_ref,
     ts_ref, left_ref, mq_ref, rloc0_ref, rloc1_ref) = refs[:9]
    if halo:
        lo_ref, hi_ref = refs[9:11]
        refs = refs[12:]
    else:
        refs = refs[9:]
    per = idx_ref.shape[2]
    tl_of = lambda t: idx_ref[t // per, 0, t % per]
    tr_of = lambda t: idx_ref[t // per, 1, t % per]
    out_ref, c_scr, x_scr, y_scr, kron_scr = refs
    first_step = pl.program_id(0) == 0
    i = base + pl.program_id(0) * stride
    gi = ids_ref[0, 0] + i

    def size_at(shift):
        j = gi + shift
        inside = (j >= 0) & (j < total)
        return jnp.where(inside, bs_ref[jnp.clip(j, 0, total - 1)], 0)

    sloc = [sh_ref[ids_ref[0, 1] + p] for p in range(npl)]
    depth = ts_ref.shape[-1]
    nq = ts_ref.shape[1]
    rows = lax.broadcasted_iota(jnp.int32, (depth, depth), 0)
    cols = lax.broadcasted_iota(jnp.int32, (depth, depth), 1)
    row_ok = rows < bs_ref[gi]
    for q in range(nq):
        keep = row_ok & (cols < size_at(sh_ref[q]))
        c_scr[q] = jnp.where(keep, ts_ref[0, q], jnp.zeros_like(ts_ref[0, q]))

    nr = npl * nt
    rchunk = RCHUNK

    @pl.when(first_step)
    def _():
        a = lax.broadcasted_iota(jnp.int32, (nr * YT, nr), 0)
        r = lax.broadcasted_iota(jnp.int32, (nr * YT, nr), 1)
        pick = jnp.where(a // YT == r, 1.0, 0.0).astype(mq_ref.dtype)
        rep = jnp.dot(pick, mq_ref[...], preferred_element_type=jnp.float32)
        ra = lax.broadcasted_iota(jnp.int32, rep.shape, 0)
        cb = lax.broadcasted_iota(jnp.int32, rep.shape, 1)
        kron_scr[...] = jnp.where(ra % YT == cb % YT, rep, 0.0).astype(kron_scr.dtype)

    for yb in range(0 if "nomix" in VARIANT else depth // (2 * YT)):
        ya, yc = 2 * yb * YT, (2 * yb + 1) * YT
        cy = jnp.concatenate(
            [c_scr[:, ya:ya + YT, :].reshape(nq * YT, depth),
             c_scr[:, yc:yc + YT, :].reshape(nq * YT, depth)], axis=1)
        for rc in range(nr // rchunk):
            k = kron_scr[rc * rchunk * YT:(rc + 1) * rchunk * YT, :]
            xy = jnp.dot(k, cy, preferred_element_type=jnp.float32)
            for half, y0 in enumerate((ya, yc)):
                x_scr[rc * rchunk:(rc + 1) * rchunk, y0:y0 + YT, :] = (
                    xy[:, half * depth:(half + 1) * depth]
                    .reshape(rchunk, YT, depth).astype(x_scr.dtype))

    def left_step(t, carry):
        lt = left_ref[tl_of(t), 0]
        xs = jnp.concatenate([x_scr[t * npl + p] for p in range(npl)], axis=1)
        yt = jnp.dot(lt, xs, preferred_element_type=jnp.float32).astype(y_scr.dtype)
        for p in range(npl):
            y_scr[p, t] = yt[:, p * depth:(p + 1) * depth]
        return carry

    if "noleft" not in VARIANT:
        lax.fori_loop(0, nt, left_step, 0, unroll=UNROLL)

    def right_sum(p, src):
        def step(u, acc):
            ts_ = [RG * u + g for g in range(RG)]
            lhs = jnp.concatenate([y_scr[p, t] for t in ts_], axis=1)
            rhs = jnp.concatenate([src[tr_of(t), 0] for t in ts_], axis=0)
            return acc + jnp.dot(lhs, rhs, preferred_element_type=jnp.float32)
        acc = lax.fori_loop(0, nt // RG, step, jnp.zeros((depth, depth), jnp.float32),
                            unroll=RUNROLL)
        keep = row_ok & (cols < size_at(sloc[p]))
        out_ref[0, p] = jnp.where(keep, acc, 0.0).astype(out_ref.dtype)

    for p, rloc in enumerate(() if "noright" in VARIANT else (rloc0_ref, rloc1_ref)):
        if not halo:
            right_sum(p, rloc)
            continue
        j = i + sloc[p]

        @pl.when(j < 0)
        def _():
            right_sum(p, lo_ref)

        @pl.when((j >= 0) & (j < nb))
        def _():
            right_sum(p, rloc)

        @pl.when(j >= nb)
        def _():
            right_sum(p, hi_ref)


def gather_kernel(nm, x_ref, idx_ref, out_ref, idx_out_ref, send_sem, recv_sem,
                  isend_sem, irecv_sem):
    me = lax.axis_index("mpo")
    barrier = pltpu.get_barrier_semaphore()
    for d in range(1, nm):
        pl.semaphore_signal(barrier, inc=1, device_id={"mpo": lax.rem(me + d, nm)},
                            device_id_type=pl.DeviceIdType.MESH)
    pl.semaphore_wait(barrier, nm - 1)
    copies = []
    for d in range(1, nm):
        peer = lax.rem(me + d, nm)
        for src, dst, ssem, rsem in ((x_ref.at[peer], out_ref.at[me], send_sem, recv_sem),
                                     (idx_ref, idx_out_ref.at[me], isend_sem, irecv_sem)):
            copy = pltpu.make_async_remote_copy(
                src_ref=src,
                dst_ref=dst,
                send_sem=ssem.at[d],
                recv_sem=rsem.at[d],
                device_id={"mpo": peer},
                device_id_type=pl.DeviceIdType.MESH,
            )
            copy.start()
            copies.append(copy)
    out_ref[me] = x_ref[me]
    idx_out_ref[me] = idx_ref[...]
    for copy in copies:
        copy.wait()


def gather_terms(rows, idx):
    nm = lax.axis_size("mpo")
    sems = [pltpu.SemaphoreType.DMA((nm,)) for _ in range(4)]
    return pl.pallas_call(
        functools.partial(gather_kernel, nm),
        out_shape=(jax.ShapeDtypeStruct(rows.shape, rows.dtype),
                   jax.ShapeDtypeStruct((nm,) + idx.shape, idx.dtype)),
        in_specs=[pl.BlockSpec(memory_space=pltpu.VMEM)] * 2,
        out_specs=(pl.BlockSpec(memory_space=pltpu.VMEM),) * 2,
        scratch_shapes=sems,
        compiler_params=pltpu.CompilerParams(collective_id=0, has_side_effects=True),
    )(rows, idx)


def edge_kernel(width, npl, src_ref, head_ref, tail_ref, ids_ref, sem):
    lane = lax.broadcasted_iota(jnp.int32, ids_ref.shape, 1)
    first = lax.axis_index("blk") * src_ref.shape[1]
    ids_ref[...] = jnp.where(lane == 0, first, lax.axis_index("mpo") * npl).astype(jnp.int32)
    last = src_ref.shape[1] - width
    copies = [pltpu.make_async_copy(src_ref.at[:, pl.ds(0, width)], head_ref, sem.at[0]),
              pltpu.make_async_copy(src_ref.at[:, pl.ds(last, width)], tail_ref, sem.at[1])]
    for copy in copies:
        copy.start()
    for copy in copies:
        copy.wait()


def edges(cells, width, npl):
    shape = (cells.shape[0], width) + cells.shape[2:]
    part = jax.ShapeDtypeStruct(shape, cells.dtype)
    return pl.pallas_call(
        functools.partial(edge_kernel, width, npl),
        out_shape=(part, part, jax.ShapeDtypeStruct((1, 128), jnp.int32)),
        in_specs=[pl.BlockSpec(memory_space=pl.ANY)],
        out_specs=(pl.BlockSpec(memory_space=pltpu.VMEM),) * 3,
        scratch_shapes=[pltpu.SemaphoreType.DMA((2,))],
    )(cells)


def halos(cells, axis, dim, width, npl):
    count = lax.axis_size(axis)
    ends = count - 1
    head, tail, ids = edges(cells, width, npl)
    lo = lax.ppermute(tail, axis, [(i, i + 1) for i in range(ends)])
    hi = lax.ppermute(head, axis, [(i + 1, i) for i in range(ends)])
    return lo, hi, ids


def body(two_site, left_env, right_env, mpo_terms, term_left, term_right, shifts, block_sizes):
    blocks, nq, depth, _ = two_site.shape
    width = left_env.shape[0]
    nmpo = lax.axis_size("mpo")
    npl = nq // nmpo
    total = blocks * lax.axis_size("blk")
    first = lax.axis_index("blk") * blocks
    p_first = lax.axis_index("mpo") * npl

    local_terms = mpo_terms.shape[0]
    rows = mpo_terms.reshape(local_terms, nmpo, npl, nq).transpose(1, 0, 2, 3)
    rows = jnp.repeat(rows.reshape(nmpo, local_terms * npl, nq), YT, axis=2)
    idx = jnp.stack([term_left, term_right]).astype(jnp.int32)
    mq, idx = gather_terms(rows, idx)
    nt = nmpo * local_terms
    mq = mq.reshape(nt * npl, nq * YT)

    lo, hi, ids = halos(right_env, "blk", 1, SH, npl)

    scalars = (idx, block_sizes, shifts, ids)
    inner = block_call(*scalars, two_site, left_env, mq, right_env, None, None, None, npl=npl)
    return block_call(*scalars, two_site, left_env, mq, right_env, lo, hi, inner, npl=npl)


def block_call(idx, block_sizes, shifts, ids, two_site, left_env, mq, right_env,
               lo, hi, prev, npl):
    blocks, nq, depth, _ = two_site.shape
    total = block_sizes.shape[0]
    halo = prev is not None
    if halo:
        base, stride, steps = 0, blocks - 1, 2
    else:
        base, stride, steps = 1, 1, blocks - 2
    width = left_env.shape[0]
    nt = idx.shape[0] * idx.shape[2]
    rblock = (width, 1, depth, depth)

    def rloc_map(p):
        def index(b, idx_r, bs_r, sh_r, ids_r):
            return (0, jnp.clip(base + b * stride + sh_r[ids_r[0, 1] + p], 0, blocks - 1), 0, 0)
        return index

    const4 = lambda b, *refs: (0, 0, 0, 0)
    in_specs = [
        pl.BlockSpec((1, nq, depth, depth), lambda b, *refs: (base + b * stride, 0, 0, 0)),
        pl.BlockSpec(rblock, lambda b, *refs: (0, base + b * stride, 0, 0)),
        pl.BlockSpec(mq.shape, lambda b, *refs: (0, 0)),
        pl.BlockSpec(rblock, rloc_map(0)),
        pl.BlockSpec(rblock, rloc_map(1)),
    ]
    operands = [two_site, left_env, mq, right_env, right_env]
    aliases = {}
    if halo:
        in_specs += [pl.BlockSpec(memory_space=pltpu.VMEM), pl.BlockSpec(memory_space=pltpu.VMEM),
                     pl.BlockSpec(memory_space=pl.ANY)]
        operands += [lo, hi, prev]
        aliases = {4 + len(operands) - 1: 0}
    grid_spec = pltpu.PrefetchScalarGridSpec(
        num_scalar_prefetch=4,
        grid=(steps,),
        in_specs=in_specs,
        out_specs=pl.BlockSpec((1, npl, depth, depth),
                               lambda b, *refs: (base + b * stride, 0, 0, 0)),
        scratch_shapes=[
            pltpu.VMEM((nq, depth, depth), jnp.bfloat16),
            pltpu.VMEM((nt * npl, depth, depth), jnp.bfloat16),
            pltpu.VMEM((npl, nt, depth, depth), jnp.bfloat16),
            pltpu.VMEM((nt * npl * YT, nq * YT), jnp.bfloat16),
        ],
    )
    flops = 2 * steps * (nt * npl * YT * nq * YT * depth + 2 * nt * npl * depth ** 3)
    return pl.pallas_call(
        functools.partial(kernel, npl, nt, base, stride, blocks, total, halo),
        out_shape=jax.ShapeDtypeStruct((blocks, npl, depth, depth), jnp.bfloat16),
        grid_spec=grid_spec,
        compiler_params=pltpu.CompilerParams(
            dimension_semantics=("arbitrary",), vmem_limit_bytes=(48 if halo else 60) * 1024 * 1024),
        cost_estimate=pl.CostEstimate(
            flops=flops, transcendentals=0,
            bytes_accessed=2 * steps * (two_site.size + left_env.size + 3 * right_env.size)
            // blocks),
        input_output_aliases=aliases,
    )(idx, block_sizes, shifts, ids, *operands)


def solution(mesh):
    return jax.shard_map(
        body,
        mesh=mesh,
        in_specs=(
            P("blk", None, None, None),
            P(None, "blk", None, None),
            P(None, "blk", None, None),
            P("mpo", None, None),
            P("mpo"),
            P("mpo"),
            P(),
            P(),
        ),
        out_specs=P("blk", "mpo", None, None),
        check_vma=False,
    )
```
